256 devices in a mesh: row: 16 (over x_lo, z), col: 16 (over y, x_hi, core).
Axes of the slice: x: 4 (x_hi: 2, x_lo: 2; x = x_hi * 2 + x_lo), y: 4, z: 8, core: 2. Of those that a mesh axis runs over, the one named last changes fastest.
Arguments:
- features: bfloat16 [1024, 1024, 128], P('row', 'col'), may hold values from -6 to 6
- kernels: bfloat16 [2, 3, 3, 128, 128], replicated, may hold values from -0.1875 to 0.1875
- length: int32 [1], replicated, may hold values from 512 to 1024
- cotangent: bfloat16 [1024, 1024, 128], P('row', 'col'), may hold values from -6 to 6
Outputs:
- output_map: bfloat16 [1024, 1024, 128], P('row', 'col')
- feature_grad: bfloat16 [1024, 1024, 128], P('row', 'col')
- kernel_gradient: float32 [2, 3, 3, 128, 128], replicated
The draws below stay inside these ranges and needn't reach their ends.
Inputs may be any that keep to these rules, and one draw needn't show every extreme that they name: The protein occupies the first length rows and columns of the pair map.
All inputs are finite; a program needn't handle non-finite values.
Results may differ from the reference program's by a relative error of at most 0.0039.
Values may be sent and summed in bfloat16 or wider, within the bound.
A program may use at most 192 MiB of HBM per device.

```python
import jax
import jax.numpy as jnp
from jax import lax

C = 128
FIRST_SPACING = 4
SECOND_SPACING = 8
N = 1024


def block_levels(key, dims, cuts, low, largest):
    def one(position, blocks):
        heights = jax.random.uniform(jax.random.fold_in(jax.random.fold_in(key, 6), position), (blocks,), jnp.float32, low / len(cuts), largest / len(cuts))
        return jnp.repeat(jnp.exp(heights), dims[position] // blocks).reshape((-1,) + (1,) * (len(dims) - position - 1))

    gain = one(*cuts[0])
    for cut in cuts[1:]:
        gain = gain * one(*cut)
    return gain


def scatter_about(key, extent, scale, most, shards=(), kind=jnp.bfloat16):
    level = block_levels(key, extent, shards, -0.22, 0.18) if shards else 1.0
    drawn = jax.random.normal(key, extent, jnp.float32) * scale * level
    return jnp.minimum(jnp.maximum(drawn, -most), most).astype(kind)


def setup_inputs(seed: int = 0) -> dict:
    key_of = jax.random.split(jax.random.key(seed), 5)
    return {
        "features": scatter_about(key_of[0], (N, N, C), 1.0, 6.0, ((0, 16), (1, 16))),
        "kernels": scatter_about(key_of[1], (2, 3, 3, C, C), (9 * C) ** -0.5, 0.1875),
        "length": jax.random.randint(key_of[2], (1,), N // 2, N + 1).astype(jnp.int32),
        "cotangent": scatter_about(key_of[3], (N, N, C), 1.0, 6.0, ((0, 16), (1, 16))),
    }


def elu_value(values):
    return jnp.where(values > 0, values, jnp.expm1(jnp.minimum(values, 0.0)))


def elu_slope(values):
    return jnp.where(values > 0, 1.0, jnp.exp(jnp.minimum(values, 0.0)))


def spaced_kernel(inputs, kernel, dilation):
    result = lax.conv_general_dilated(inputs.astype(jnp.float32)[None], kernel.astype(jnp.float32), (1, 1), ((dilation, dilation), (dilation, dilation)), rhs_dilation=(dilation, dilation), dimension_numbers=("NHWC", "HWIO", "NHWC"), precision=lax.Precision.HIGHEST)
    return result[0]


def reversed_kernel(kernel):
    return kernel[::-1, ::-1].transpose(0, 1, 3, 2)


def kernel_contributions(acts, grads, dilation):
    padded = jnp.pad(acts.astype(jnp.float32), ((dilation, dilation), (dilation, dilation), (0, 0)))
    flat_grads = grads.astype(jnp.float32).reshape(-1, C)
    pieces = []
    for p in range(3):
        for q in range(3):
            window = padded[p * dilation:p * dilation + N, q * dilation:q * dilation + N].reshape(-1, C)
            pieces.append(lax.dot_general(window, flat_grads, (((0,), (0,)), ((), ())), precision=lax.Precision.HIGHEST, preferred_element_type=jnp.float32))
    return jnp.stack(pieces).reshape(3, 3, C, C)


def reference(features, kernels, length, cotangent):
    limit = length[0]
    inside = jnp.arange(N) < limit
    live = (inside[:, None] & inside[None, :]).astype(jnp.float32)[:, :, None]
    initial_state = features.astype(jnp.float32)
    first_activation = (live * elu_value(initial_state)).astype(jnp.bfloat16)
    first_state = initial_state + spaced_kernel(first_activation, kernels[0], FIRST_SPACING)
    second_activation = (live * elu_value(first_state)).astype(jnp.bfloat16)
    second_state = first_state + spaced_kernel(second_activation, kernels[1], SECOND_SPACING)
    output_map = (live * second_state).astype(jnp.bfloat16)
    second_gradient = (live * cotangent.astype(jnp.float32)).astype(jnp.bfloat16)
    second_backward = spaced_kernel(second_gradient, reversed_kernel(kernels[1]), SECOND_SPACING)
    grad_full = second_gradient.astype(jnp.float32) + live * elu_slope(first_state) * second_backward
    first_gradient = grad_full.astype(jnp.bfloat16)
    first_backward = spaced_kernel(first_gradient, reversed_kernel(kernels[0]), FIRST_SPACING)
    feature_grad = (grad_full + live * elu_slope(initial_state) * first_backward).astype(jnp.bfloat16)
    kernel_gradient = jnp.stack([kernel_contributions(first_activation, first_gradient, FIRST_SPACING), kernel_contributions(second_activation, second_gradient, SECOND_SPACING)])
    kernel_gradient = kernel_gradient / limit.astype(jnp.float32)
    return output_map, feature_grad, kernel_gradient
```

```python
import functools

import jax
import jax.numpy as jnp
from jax import lax
from jax.experimental import pallas as pl
from jax.experimental.pallas import tpu as pltpu
from jax.sharding import PartitionSpec as P

MESH = pl.DeviceIdType.MESH
F32, BF16 = jnp.float32, jnp.bfloat16
FIRST_SPACING = 4
SECOND_SPACING = 8
CELL = 4
ONE, TWO = FIRST_SPACING // CELL, SECOND_SPACING // CELL
HALO = ONE + TWO
T = 16
FULL = T + 2 * HALO
WIDE = T + 2 * TWO
MID = T + 2 * ONE
LANES = 128
SIDES = [(r, c) for r in (-1, 0, 1) for c in (-1, 0, 1) if (r, c) != (0, 0)]
GROUPS = 9


def exp_low(values):
    return jnp.exp(jnp.minimum(values, 0.0))


def elu(values):
    return jnp.where(values > 0, values, exp_low(values) - 1.0)


def slope(values):
    return jnp.where(values > 0, 1.0, exp_low(values))


def place():
    i, j = lax.axis_index("row"), lax.axis_index("col")
    x_lo, z = i // 8, i % 8
    y, x_hi, core = j // 4, (j // 2) % 2, j % 2
    return i, j, x_hi * 2 + x_lo, y, z, core


def at(x, y, z, core):
    return ((x % 2) * 8 + z, y * 4 + (x // 2) * 2 + core)


def flip(value, k):
    total = 0
    for bit in (1, 2, 4):
        b = (value // bit) % 2
        total = total + bit * ((1 - b) if k & bit else b)
    return total


def fill_weights(kern, forward, backward, layer):
    zero = jnp.zeros((3 * LANES, LANES), BF16)
    for ref in (forward, backward):
        ref[0 : 3 * LANES, LANES:] = zero
        ref[9 * LANES :, :LANES] = zero
    for p in range(3):
        for q in range(3):
            k = kern[layer, p, q]
            kt = k.T
            for u in range(2):
                a = ((p + u) * 3 + q) * LANES
                forward[a : a + LANES, u * LANES : (u + 1) * LANES] = k
                b = ((2 - p + u) * 3 + 2 - q) * LANES
                backward[b : b + LANES, u * LANES : (u + 1) * LANES] = kt


def windows(ref, row, rows, s, left, width, taps=4):
    out = []
    for t in range(taps):
        for q in range(3):
            v = ref[pl.ds(row + t * s, rows), left + q * s : left + q * s + width]
            out.append(v.reshape(rows * width * 16, LANES))
    return jnp.concatenate(out, axis=1)


def pairs(ref, weights, row, s, width):
    lhs = windows(ref, row, s, s, 0, width)
    return jnp.dot(lhs, weights[...], preferred_element_type=F32)


def kernel(
    remote, f_hbm, g_hbm, kern, limit_ref, om_ref, fg_ref, kg_ref,
    f, g, a1, s1, a2, g1, gf, w1, w1b, w2, w2b, rowm, colm, dw,
    full, wire0, got0, wirex, gotx, wirey, goty, zbuf, res,
    local_sem, halo_send, halo_recv, ar_send, ar_recv,
):
    i, j, x, y, z, core = place()
    if remote:
        barrier = pltpu.get_barrier_semaphore()
        friends = [(lax.rem(i + dr + 16, 16), lax.rem(j + dc + 16, 16)) for dr, dc in SIDES]
        core_friend = [at(x, y, z, 1 - core)]
        x_friends = [at(flip(x, k), y, z, core) for k in range(1, 4)]
        y_friends = [at(x, flip(y, k), z, core) for k in range(1, 4)]
        z_friends = [at(x, y, flip(z, k), core) for k in range(1, 8)]
        everyone = friends + core_friend + x_friends + y_friends + z_friends
        for d in everyone:
            pl.semaphore_signal(barrier, inc=1, device_id=d, device_id_type=MESH)
    mid = pl.ds(HALO, T)
    local = [
        pltpu.make_async_copy(f_hbm, f.at[mid, mid], local_sem.at[0]),
        pltpu.make_async_copy(g_hbm, g.at[mid, mid], local_sem.at[1]),
    ]
    for c in local:
        c.start()
    halo = []
    if remote:
        pl.semaphore_wait(barrier, len(everyone))
        src = {-1: pl.ds(0, HALO), 0: pl.ds(0, T), 1: pl.ds(T - HALO, HALO)}
        dst = {-1: pl.ds(HALO + T, HALO), 0: mid, 1: pl.ds(0, HALO)}
        for n, (a, b) in enumerate(((f_hbm, f), (g_hbm, g))):
            for m, (dr, dc) in enumerate(SIDES):
                c = pltpu.make_async_remote_copy(
                    src_ref=a.at[src[dr], src[dc]], dst_ref=b.at[dst[dr], dst[dc]],
                    send_sem=halo_send.at[n, m], recv_sem=halo_recv.at[n, m],
                    device_id=friends[m], device_id_type=MESH,
                )
                c.start()
                halo.append(c)

    limit = limit_ref[0]
    sub = lax.broadcasted_iota(jnp.int32, (FULL, 16, LANES), 1)
    blk = (lax.broadcasted_iota(jnp.int32, (FULL, 16, LANES), 0) - HALO) * CELL
    rid = blk + sub // CELL + i * (T * CELL)
    cid = blk + sub % CELL + j * (T * CELL)
    rowm[...] = jnp.where((rid >= 0) & (rid < limit), 1.0, 0.0).astype(F32)
    colm[...] = jnp.where((cid >= 0) & (cid < limit), 1.0, 0.0).astype(F32)
    fill_weights(kern, w1, w1b, 0)
    fill_weights(kern, w2, w2b, 1)
    for c in local:
        c.wait()
    for c in halo:
        c.wait_recv()

    def first(r, _):
        m = rowm[r] * colm[...]
        a1[r] = (elu(f[r].astype(F32)) * m).astype(BF16)
        g[r] = (g[r].astype(F32) * m).astype(BF16)
        return 0

    if remote:
        for c in halo:
            c.wait_send()
    lax.fori_loop(0, FULL, first, 0)

    def conv1(k, _):
        r = 2 * k
        both = pairs(a1, w1, r, ONE, WIDE)
        for u in range(2):
            v = both[:, u * LANES : (u + 1) * LANES].reshape(WIDE, 16, LANES)
            v = v + f[r + u + 1, 1 : 1 + WIDE].astype(F32)
            s1[r + u] = v
            a2[r + u] = (elu(v) * (rowm[r + u + 1] * colm[1 : 1 + WIDE])).astype(BF16)
        return 0

    lax.fori_loop(0, WIDE // 2, conv1, 0)

    def contract(act, a_row, a_col, grad, g_at, s, layer):
        def step(k, _):
            if s == 1:
                rows = [pl.ds(k * 8 + 2 * n, 1) for n in range(4)]
            else:
                rows = [pl.ds(k * 8 + 4 * n, 2) for n in range(2)]
            base = [k * 8 + (2 if s == 1 else 4) * n for n in range(4 // s)]
            lhs, rhs = [], []
            for b in base:
                gs = [
                    grad[pl.ds(b + g_at + u * s, s), g_at : g_at + T].reshape(s * T * 16, LANES)
                    for u in range(2)
                ]
                lhs.append(jnp.concatenate(gs, axis=1))
                rhs.append(windows(act, b + a_row, s, s, a_col, T))
            lhs = jnp.concatenate(lhs, axis=0)
            rhs = jnp.concatenate(rhs, axis=0)
            part = lax.dot_general(lhs, rhs, (((0,), (0,)), ((), ())), preferred_element_type=F32)

            @pl.when(k == 0)
            def _():
                dw[...] = part

            @pl.when(k != 0)
            def _():
                dw[...] += part

            return 0

        lax.fori_loop(0, 2, step, 0)
        for p in range(3):
            for q in range(3):
                lo = (p * 3 + q) * LANES
                hi = ((p + 1) * 3 + q) * LANES
                v = dw[:LANES, lo : lo + LANES] + dw[LANES:, hi : hi + LANES]
                n = (layer * 9 + p * 3 + q) * 16
                full[n : n + 16] = v.T.reshape(16, 8, LANES)

    contract(a2, 0, 0, g, HALO, TWO, 1)

    def finish_one(r, back):
        v = back.reshape(MID, 16, LANES)
        m = rowm[r + TWO] * colm[TWO : TWO + MID]
        v = g[r + TWO, TWO : TWO + MID].astype(F32) + m * slope(s1[r + 1, 1 : 1 + MID]) * v
        gf[r] = v
        g1[r] = v.astype(BF16)

    def back2(k, _):
        r = 4 * k
        both = pairs(g, w2b, r, TWO, MID)
        n = MID * 16
        for u in range(2):
            for e in range(2):
                finish_one(r + 2 * u + e, both[e * n : (e + 1) * n, u * LANES : (u + 1) * LANES])
        return 0

    lax.fori_loop(0, T // 4, back2, 0)
    tail = jnp.dot(
        windows(g, T, MID - T, TWO, 0, MID, 3), w2b[: 9 * LANES, :LANES], preferred_element_type=F32
    )
    for e in range(MID - T):
        finish_one(T + e, tail[e * MID * 16 : (e + 1) * MID * 16])

    contract(a1, HALO - ONE, HALO - ONE, g1, ONE, ONE, 0)

    def back1(k, _):
        r = 2 * k
        both = pairs(g1, w1b, r, ONE, T)
        for u in range(2):
            v = both[:, u * LANES : (u + 1) * LANES].reshape(T, 16, LANES)
            m = rowm[r + u + HALO] * colm[HALO : HALO + T]
            o = slope(f[r + u + HALO, HALO : HALO + T].astype(F32))
            fg_ref[r + u] = (gf[r + u + ONE, ONE : ONE + T] + m * o * v).astype(BF16)
        return 0

    lax.fori_loop(0, T // 2, back1, 0)

    def conv2(k, _):
        r = 4 * k
        both = pairs(a2, w2, r, TWO, T)
        n = T * 16
        for u in range(2):
            for e in range(2):
                v = both[e * n : (e + 1) * n, u * LANES : (u + 1) * LANES].reshape(T, 16, LANES)
                row = r + 2 * u + e
                m = rowm[row + HALO] * colm[HALO : HALO + T]
                om_ref[row] = (m * (s1[row + TWO, TWO : TWO + T] + v)).astype(BF16)
        return 0

    lax.fori_loop(0, T // 4, conv2, 0)

    if not remote:
        kg_ref[...] = full[...] / limit.astype(F32)
        return

    slot = [0]

    def send(source, target, device):
        n = slot[0]
        slot[0] += 1
        c = pltpu.make_async_remote_copy(
            src_ref=source, dst_ref=target, send_sem=ar_send.at[n], recv_sem=ar_recv.at[n],
            device_id=device, device_id_type=MESH,
        )
        c.start()
        return c

    n0, nx, ny = 16 * GROUPS, 4 * GROUPS, GROUPS
    wire0[...] = full[pl.ds((1 - core) * n0, n0)].astype(wire0.dtype)
    c = send(wire0, got0, core_friend[0])
    c.wait()
    keep = full.at[pl.ds(core * n0, n0)]
    keep[...] += got0[...].astype(F32)
    wirex[...] = keep[...].astype(wirex.dtype)
    cs = [
        send(wirex.at[pl.ds(flip(x, k) * nx, nx)], gotx.at[k - 1], x_friends[k - 1])
        for k in range(1, 4)
    ]
    for c in cs:
        c.wait()
    keepx = full.at[pl.ds(core * n0 + x * nx, nx)]
    total = keepx[...]
    for k in range(3):
        total = total + gotx[k].astype(F32)
    keepx[...] = total
    wirey[...] = total.astype(wirey.dtype)
    cs = [
        send(wirey.at[pl.ds(flip(y, k) * ny, ny)], goty.at[k - 1], y_friends[k - 1])
        for k in range(1, 4)
    ]
    for c in cs:
        c.wait()
    total = full[pl.ds(core * n0 + x * nx + y * ny, ny)]
    for k in range(3):
        total = total + goty[k].astype(F32)
    zbuf[z] = total.astype(zbuf.dtype)
    cs = [send(zbuf.at[z], zbuf.at[z], z_friends[k - 1]) for k in range(1, 8)]
    for c in cs:
        c.wait()
    total = zbuf[0].astype(F32)
    for k in range(1, 8):
        total = total + zbuf[k].astype(F32)
    res[core, x, y] = (total / limit.astype(F32)).astype(res.dtype)
    mine = res.at[core, x, y]
    cs = [send(mine, mine, d) for d in y_friends]
    for c in cs:
        c.wait()
    mine = res.at[core, x]
    cs = [send(mine, mine, d) for d in x_friends]
    for c in cs:
        c.wait()
    mine = res.at[core]
    c = send(mine, mine, core_friend[0])
    c.wait()
    kg_ref[...] = res[...].astype(F32).reshape(kg_ref.shape)


def to_blocks(v):
    r, c, ch = v.shape
    return (
        v.reshape(r // CELL, CELL, c // CELL, CELL, ch)
        .transpose(0, 2, 1, 3, 4)
        .reshape(r // CELL, c // CELL, CELL * CELL, ch)
    )


def from_blocks(v):
    r, c, _, ch = v.shape
    return (
        v.reshape(r, c, CELL, CELL, ch).transpose(0, 2, 1, 3, 4).reshape(r * CELL, c * CELL, ch)
    )


WIRE = BF16


def call(remote, f, g, kernels, length):
    vm = pltpu.VMEM
    sems = pltpu.SemaphoreType.DMA
    whole = 2 * 4 * 4 * GROUPS
    om, fg, kg = pl.pallas_call(
        functools.partial(kernel, remote),
        out_shape=(
            jax.ShapeDtypeStruct((T, T, 16, LANES), BF16),
            jax.ShapeDtypeStruct((T, T, 16, LANES), BF16),
            jax.ShapeDtypeStruct((whole, 8, LANES), F32),
        ),
        in_specs=[
            pl.BlockSpec(memory_space=pl.ANY),
            pl.BlockSpec(memory_space=pl.ANY),
            pl.BlockSpec(memory_space=pltpu.VMEM),
            pl.BlockSpec(memory_space=pltpu.SMEM),
        ],
        out_specs=[pl.BlockSpec(memory_space=pltpu.VMEM)] * 3,
        scratch_shapes=[
            vm((FULL, FULL, 16, LANES), BF16),
            vm((FULL, FULL, 16, LANES), BF16),
            vm((FULL, FULL, 16, LANES), BF16),
            vm((WIDE, WIDE, 16, LANES), F32),
            vm((WIDE, WIDE, 16, LANES), BF16),
            vm((MID, MID, 16, LANES), BF16),
            vm((MID, MID, 16, LANES), F32),
            vm((12 * LANES, 2 * LANES), BF16),
            vm((12 * LANES, 2 * LANES), BF16),
            vm((12 * LANES, 2 * LANES), BF16),
            vm((12 * LANES, 2 * LANES), BF16),
            vm((FULL, 16, LANES), F32),
            vm((FULL, 16, LANES), F32),
            vm((2 * LANES, 12 * LANES), F32),
            vm((whole, 8, LANES), F32),
            vm((16 * GROUPS, 8, LANES), WIRE),
            vm((16 * GROUPS, 8, LANES), WIRE),
            vm((16 * GROUPS, 8, LANES), WIRE),
            vm((3, 4 * GROUPS, 8, LANES), WIRE),
            vm((4 * GROUPS, 8, LANES), WIRE),
            vm((3, GROUPS, 8, LANES), WIRE),
            vm((8, GROUPS, 8, LANES), WIRE),
            vm((2, 4, 4, GROUPS, 8, LANES), WIRE),
            sems((2,)),
            sems((2, 8)),
            sems((2, 8)),
            sems((21,)),
            sems((21,)),
        ],
        compiler_params=pltpu.CompilerParams(
            collective_id=0 if remote else None, has_side_effects=True, vmem_limit_bytes=60 << 20
        ),
    )(f, g, kernels, length)
    return om, fg, kg


def body(features, kernels, length, cotangent):
    om, fg, kg = call(True, to_blocks(features), to_blocks(cotangent), kernels, length)
    return from_blocks(om), from_blocks(fg), kg.reshape(kernels.shape)


def solution(mesh):
    in_specs = (P("row", "col", None), P(), P(), P("row", "col", None))
    out_specs = (P("row", "col", None), P("row", "col", None), P())
    return jax.shard_map(body, mesh=mesh, in_specs=in_specs, out_specs=out_specs, check_vma=False)
```

```python
import functools

import jax
import jax.numpy as jnp
from jax import lax
from jax.experimental import pallas as pl
from jax.experimental.pallas import tpu as pltpu
from jax.sharding import PartitionSpec as P

MESH = pl.DeviceIdType.MESH
F32, BF16 = jnp.float32, jnp.bfloat16
FIRST_SPACING = 4
SECOND_SPACING = 8
CELL = 4
ONE, TWO = FIRST_SPACING // CELL, SECOND_SPACING // CELL
T = 16
LANES = 128
SIDES = [(r, c) for r in (-1, 0, 1) for c in (-1, 0, 1) if (r, c) != (0, 0)]
HALF = 72
PIECE = 5
PADDED = 16 * PIECE
WIRE = BF16


def exp_low(values):
    return jnp.exp(jnp.minimum(values, 0.0))


def elu(values):
    return jnp.where(values > 0, values, exp_low(values) - 1.0)


def slope(values):
    return jnp.where(values > 0, 1.0, exp_low(values))


def place():
    i, j = lax.axis_index("row"), lax.axis_index("col")
    x_lo, z = i // 8, i % 8
    y, x_hi, core = j // 4, (j // 2) % 2, j % 2
    return i, j, x_hi * 2 + x_lo, y, z, core


def at(x, y, z, core):
    return ((x % 2) * 8 + z, y * 4 + (x // 2) * 2 + core)


def flip(value, k):
    total = 0
    for bit in (1, 2, 4):
        b = (value // bit) % 2
        total = total + bit * ((1 - b) if k & bit else b)
    return total


def fill_weights(kern, forward, backward, layer):
    zero = jnp.zeros((3 * LANES, LANES), BF16)
    for ref in (forward, backward):
        ref[0 : 3 * LANES, LANES:] = zero
        ref[9 * LANES :, :LANES] = zero
    for p in range(3):
        for q in range(3):
            k = kern[layer, p, q]
            kt = k.T
            for u in range(2):
                a = ((p + u) * 3 + q) * LANES
                forward[a : a + LANES, u * LANES : (u + 1) * LANES] = k
                b = ((2 - p + u) * 3 + 2 - q) * LANES
                backward[b : b + LANES, u * LANES : (u + 1) * LANES] = kt


def windows(ref, row, s, left=0):
    out = []
    for t in range(4):
        for q in range(3):
            v = ref[pl.ds(row + t * s, s), left + q * s : left + q * s + T]
            out.append(v.reshape(s * T * 16, LANES))
    return jnp.concatenate(out, axis=1)


def stacked(ref, row, s, rows):
    return jnp.concatenate(
        [windows(ref, row + 2 * s * n, s) for n in range(rows // (2 * s))], axis=0
    )


def convolve(ref, weights, row, s, rows):
    both = jnp.dot(stacked(ref, row, s, rows), weights[...], preferred_element_type=F32)
    out = []
    m = T * 16
    for r in range(rows):
        n, u, e = r // (2 * s), (r // s) % 2, r % s
        at0 = (n * s + e) * m
        out.append(both[at0 : at0 + m, u * LANES : (u + 1) * LANES].reshape(T, 16, LANES))
    return out


def swap(low, n0, n1):
    return jnp.where(low, n0, pltpu.roll(n1, 4, 1)), jnp.where(low, pltpu.roll(n0, 4, 1), n1)


def low_half():
    return lax.broadcasted_iota(jnp.int32, (T // 2, 8, LANES), 1) < 4


def into_blocks(ref, c):
    low = low_half()
    n = [ref[CELL * c + e].astype(F32).reshape(T // 2, 8, LANES) for e in range(4)]
    lo = swap(low, n[0], n[1])
    hi = swap(low, n[2], n[3])
    both = [jnp.concatenate([lo[k], hi[k]], axis=1) for k in range(2)]
    return jnp.stack(both, axis=1).reshape(T, 16, LANES)


def out_of_blocks(ref, c, v):
    low = low_half()
    v = v.reshape(T // 2, 2, 16, LANES)
    for h in range(2):
        part = swap(low, v[:, 0, 8 * h : 8 * h + 8], v[:, 1, 8 * h : 8 * h + 8])
        for k in range(2):
            ref[CELL * c + 2 * h + k] = part[k].reshape(T * CELL, LANES).astype(ref.dtype)


def kernel(
    remote, f_hbm, g_hbm, kern, limit_ref, om_hbm, fg_hbm, res,
    fn, gn, f, a1, s1, a2, g2, g1, gf, w1, w1b, w2, w2b, rowm, colm, dw,
    full, got0, wxy, gxy, zbuf,
    local_sem, halo_send, halo_recv, ar_send, ar_recv,
):
    i, j, x, y, z, core = place()
    friends = [(lax.rem(i + dr + 16, 16), lax.rem(j + dc + 16, 16)) for dr, dc in SIDES]
    core_friend = at(x, y, z, 1 - core)
    z_friends = [at(x, y, flip(z, k), core) for k in range(1, 8)]
    xy = [(flip(x, k // 4), flip(y, k % 4)) for k in range(1, 16)]
    xy_friends = [at(a, b, z, core) for a, b in xy]
    if remote:
        barrier = pltpu.get_barrier_semaphore()
        everyone = friends + [core_friend] + z_friends + xy_friends
        for d in everyone:
            pl.semaphore_signal(barrier, inc=1, device_id=d, device_id_type=MESH)
    local = [
        pltpu.make_async_copy(f_hbm, fn, local_sem.at[0]),
        pltpu.make_async_copy(g_hbm, gn, local_sem.at[1]),
    ]
    for c in local:
        c.start()
    started = []

    def send(source, target, send_sem, recv_sem, device):
        c = pltpu.make_async_remote_copy(
            src_ref=source, dst_ref=target, send_sem=send_sem, recv_sem=recv_sem,
            device_id=device, device_id_type=MESH,
        )
        c.start()
        started.append(c)
        return c

    def exchange(n, ref, h):
        if not remote:
            return lambda: None
        src = {-1: pl.ds(h, h), 0: pl.ds(h, T), 1: pl.ds(T, h)}
        dst = {-1: pl.ds(h + T, h), 0: pl.ds(h, T), 1: pl.ds(0, h)}
        copies = [
            send(
                ref.at[src[dr], src[dc]], ref.at[dst[dr], dst[dc]],
                halo_send.at[n, m], halo_recv.at[n, m], friends[m],
            )
            for m, (dr, dc) in enumerate(SIDES)
        ]

        def finish():
            for c in copies:
                c.wait_recv()
            strips = [
                (i == 0, pl.ds(0, h), pl.ds(0, T + 2 * h)),
                (i == 15, pl.ds(T + h, h), pl.ds(0, T + 2 * h)),
                (j == 0, pl.ds(0, T + 2 * h), pl.ds(0, h)),
                (j == 15, pl.ds(0, T + 2 * h), pl.ds(T + h, h)),
            ]
            for edge, r, c in strips:

                @pl.when(edge)
                def _():
                    ref[r, c] = jnp.zeros((r.size, c.size, 16, LANES), BF16)

        return finish

    limit = limit_ref[0]
    sub = lax.broadcasted_iota(jnp.int32, (T, 16, LANES), 1)
    blk = lax.broadcasted_iota(jnp.int32, (T, 16, LANES), 0) * CELL
    rowm[...] = jnp.where(blk + sub // CELL + i * (T * CELL) < limit, 1.0, 0.0).astype(F32)
    colm[...] = jnp.where(blk + sub % CELL + j * (T * CELL) < limit, 1.0, 0.0).astype(F32)
    own1, own2 = pl.ds(ONE, T), pl.ds(TWO, T)

    def prepare_f(c, _):
        v = into_blocks(fn, c)
        f[c] = v.astype(BF16)
        a1[c + ONE, own1] = (elu(v) * (rowm[c] * colm[...])).astype(BF16)
        return 0

    def prepare_g(c, _):
        v = into_blocks(gn, c)
        g2[c + TWO, own2] = (v * (rowm[c] * colm[...])).astype(BF16)
        return 0

    local[0].wait()
    lax.fori_loop(0, T, prepare_f, 0)
    local[1].wait()
    lax.fori_loop(0, T, prepare_g, 0)
    if remote:
        pl.semaphore_wait(barrier, len(everyone))
    finish_a1 = exchange(0, a1, ONE)
    finish_g2 = exchange(1, g2, TWO)
    fill_weights(kern, w1, w1b, 0)
    fill_weights(kern, w2, w2b, 1)

    def conv1(k, _):
        for e, v in enumerate(convolve(a1, w1, k * R, ONE, R)):
            r = k * R + e
            v = v + f[r].astype(F32)
            s1[r] = v
            a2[r + TWO, own2] = (elu(v) * (rowm[r] * colm[...])).astype(BF16)
        return 0

    finish_a1()
    lax.fori_loop(0, T // R, conv1, 0)
    finish_a2 = exchange(2, a2, TWO)

    def contract(own, o, wide, s, layer, turned):
        def step(k, _):
            lhs = []
            for n in range(8 // (2 * s)):
                b = k * 8 + 2 * s * n
                gs = [
                    own[pl.ds(b + o + u * s, s), o : o + T].reshape(s * T * 16, LANES)
                    for u in range(2)
                ]
                lhs.append(jnp.concatenate(gs, axis=1))
            lhs = jnp.concatenate(lhs, axis=0)
            rhs = stacked(wide, k * 8, s, 8)
            part = lax.dot_general(lhs, rhs, (((0,), (0,)), ((), ())), preferred_element_type=F32)

            @pl.when(k == 0)
            def _():
                dw[...] = part

            @pl.when(k != 0)
            def _():
                dw[...] += part

            return 0

        lax.fori_loop(0, 2, step, 0)
        for p in range(3):
            for q in range(3):
                a, b = (p, q) if turned else (2 - p, 2 - q)
                lo = (a * 3 + b) * LANES
                hi = ((a + 1) * 3 + b) * LANES
                v = dw[:LANES, lo : lo + LANES] + dw[LANES:, hi : hi + LANES]
                v = (v.T if turned else v).reshape(2, 8, 8, LANES)
                for h in range(2):
                    n = (p * 3 + q) * 16 + 8 * h
                    full[layer, n // HALF, n % HALF : n % HALF + 8] = v[h]
        full[layer, :, HALF:] = jnp.zeros((2, PADDED - HALF, 8, LANES), F32)

    mine = x * 4 + y
    mine_at = pl.ds(mine * PIECE, PIECE)

    class Reduction:
        def __init__(self, layer):
            self.layer, self.slot, self.pending = layer, 0, []

        def send(self, source, target, device):
            n = self.slot
            self.slot += 1
            sems = ar_send.at[self.layer, n], ar_recv.at[self.layer, n]
            self.pending.append(send(source, target, *sems, device))

        def arrive(self):
            for c in self.pending:
                c.wait_recv()
            self.pending = []

        def core_out(self):
            n = self.layer
            if remote:
                self.send(full.at[n, 1 - core], got0.at[n], core_friend)

        def plane_out(self):
            n = self.layer
            if not remote:
                return
            self.arrive()
            v = full[n, core] + got0[n]
            full[n, core] = v
            wxy[n] = v.reshape(16, PIECE, 8, LANES).astype(WIRE)
            for k, (a, b) in enumerate(xy):
                self.send(wxy.at[n, a * 4 + b], gxy.at[n, k], xy_friends[k])

        def z_out(self):
            n = self.layer
            if not remote:
                return
            self.arrive()
            v = full[n, core, mine_at]
            for k in range(15):
                v = v + gxy[n, k].astype(F32)
            zbuf[n, z] = v.astype(WIRE)
            for d in z_friends:
                self.send(zbuf.at[n, z], zbuf.at[n, z], d)

        def plane_back(self):
            n = self.layer
            if not remote:
                return
            self.arrive()
            v = zbuf[n, 0].astype(F32)
            for k in range(1, 8):
                v = v + zbuf[n, k].astype(F32)
            res[n, core, mine_at] = (v / limit.astype(F32)).astype(WIRE)
            piece = res.at[n, core, mine_at]
            for d in xy_friends:
                self.send(piece, piece, d)

        def core_back(self):
            n = self.layer
            if not remote:
                res[n] = (full[n] / limit.astype(F32)).astype(WIRE)
                return
            self.arrive()
            self.send(res.at[n, core], res.at[n, core], core_friend)

    second, first = Reduction(1), Reduction(0)

    finish_g2()
    contract(a2, TWO, g2, TWO, 1, False)
    second.core_out()

    def back2(k, _):
        for e, v in enumerate(convolve(g2, w2b, k * R, TWO, R)):
            r = k * R + e
            m = rowm[r] * colm[...]
            v = g2[r + TWO, own2].astype(F32) + m * slope(s1[r]) * v
            gf[r] = v
            g1[r + ONE, own1] = v.astype(BF16)
        return 0

    lax.fori_loop(0, T // R // 2, back2, 0)
    second.plane_out()
    lax.fori_loop(T // R // 2, T // R, back2, 0)
    finish_g1 = exchange(3, g1, ONE)
    contract(g1, ONE, a1, ONE, 0, True)
    first.core_out()
    second.z_out()
    first.plane_out()

    def conv2(k, _):
        for e, v in enumerate(convolve(a2, w2, k * R, TWO, R)):
            r = k * R + e
            out_of_blocks(fn, r, rowm[r] * colm[...] * (s1[r] + v))
        return 0

    finish_a2()
    lax.fori_loop(0, T // R, conv2, 0)
    om = pltpu.make_async_copy(fn, om_hbm, local_sem.at[2])
    om.start()
    second.plane_back()

    def back1(k, _):
        for e, v in enumerate(convolve(g1, w1b, k * R, ONE, R)):
            r = k * R + e
            m = rowm[r] * colm[...]
            out_of_blocks(gn, r, gf[r] + m * slope(f[r].astype(F32)) * v)
        return 0

    finish_g1()
    lax.fori_loop(0, T // R // 2, back1, 0)
    first.z_out()
    lax.fori_loop(T // R // 2, T // R, back1, 0)
    fg = pltpu.make_async_copy(gn, fg_hbm, local_sem.at[3])
    fg.start()
    second.core_back()
    first.plane_back()
    second.arrive()
    first.core_back()
    om.wait()
    fg.wait()
    first.arrive()
    for c in started:
        c.wait_send()


R = 4


def call(remote, f, g, kernels, length):
    vm = pltpu.VMEM
    sems = pltpu.SemaphoreType.DMA
    tile = (T * CELL, T * CELL, LANES)

    def blocks(h, kind):
        return vm((T + 2 * h, T + 2 * h, 16, LANES), kind)

    return pl.pallas_call(
        functools.partial(kernel, remote),
        out_shape=(
            jax.ShapeDtypeStruct(tile, BF16),
            jax.ShapeDtypeStruct(tile, BF16),
            jax.ShapeDtypeStruct((2, 2, PADDED, 8, LANES), WIRE),
        ),
        in_specs=[
            pl.BlockSpec(memory_space=pl.ANY),
            pl.BlockSpec(memory_space=pl.ANY),
            pl.BlockSpec(memory_space=pltpu.VMEM),
            pl.BlockSpec(memory_space=pltpu.SMEM),
        ],
        out_specs=[
            pl.BlockSpec(memory_space=pl.ANY),
            pl.BlockSpec(memory_space=pl.ANY),
            pl.BlockSpec(memory_space=pltpu.VMEM),
        ],
        scratch_shapes=[
            vm(tile, BF16),
            vm(tile, BF16),
            blocks(0, BF16),
            blocks(ONE, BF16),
            blocks(0, F32),
            blocks(TWO, BF16),
            blocks(TWO, BF16),
            blocks(ONE, BF16),
            blocks(0, F32),
            vm((12 * LANES, 2 * LANES), BF16),
            vm((12 * LANES, 2 * LANES), BF16),
            vm((12 * LANES, 2 * LANES), BF16),
            vm((12 * LANES, 2 * LANES), BF16),
            vm((T, 16, LANES), F32),
            vm((T, 16, LANES), F32),
            vm((2 * LANES, 12 * LANES), F32),
            vm((2, 2, PADDED, 8, LANES), F32),
            vm((2, PADDED, 8, LANES), F32),
            vm((2, 16, PIECE, 8, LANES), WIRE),
            vm((2, 15, PIECE, 8, LANES), WIRE),
            vm((2, 8, PIECE, 8, LANES), WIRE),
            sems((4,)),
            sems((4, 8)),
            sems((4, 8)),
            sems((2, 39)),
            sems((2, 39)),
        ],
        compiler_params=pltpu.CompilerParams(
            collective_id=0 if remote else None, has_side_effects=True, vmem_limit_bytes=60 << 20
        ),
    )(f, g, kernels, length)


def body(features, kernels, length, cotangent):
    om, fg, kg = call(True, features, cotangent, kernels, length)
    kg = kg[:, :, :HALF].astype(F32).reshape(kernels.shape)
    return om, fg, kg


def solution(mesh):
    in_specs = (P("row", "col", None), P(), P(), P("row", "col", None))
    out_specs = (P("row", "col", None), P("row", "col", None), P())
    return jax.shard_map(body, mesh=mesh, in_specs=in_specs, out_specs=out_specs, check_vma=False)
```

```python
import functools

import jax
import jax.numpy as jnp
from jax import lax
from jax.experimental import pallas as pl
from jax.experimental.pallas import tpu as pltpu
from jax.sharding import PartitionSpec as P

MESH = pl.DeviceIdType.MESH
F32, BF16 = jnp.float32, jnp.bfloat16
FIRST_SPACING = 4
SECOND_SPACING = 8
CELL = 4
ONE, TWO = FIRST_SPACING // CELL, SECOND_SPACING // CELL
T = 16
LANES = 128
SIDES = [(r, c) for r in (-1, 0, 1) for c in (-1, 0, 1) if (r, c) != (0, 0)]
HALF = 72
PIECE = 5
PADDED = 16 * PIECE
WIRE = BF16
HOPS = [(0, 1, 2, 1)[k // 4] + (0, 1, 2, 1)[k % 4] for k in range(1, 16)]


def exp_low(values):
    return jnp.exp(jnp.minimum(values, 0.0))


def elu(values):
    return jnp.where(values > 0, values, exp_low(values) - 1.0)


def slope(values):
    return jnp.where(values > 0, 1.0, exp_low(values))


def place():
    i, j = lax.axis_index("row"), lax.axis_index("col")
    x_lo, z = i // 8, i % 8
    y, x_hi, core = j // 4, (j // 2) % 2, j % 2
    return i, j, x_hi * 2 + x_lo, y, z, core


def at(x, y, z, core):
    return ((x % 2) * 8 + z, y * 4 + (x // 2) * 2 + core)


def flip(value, k):
    total = 0
    for bit in (1, 2, 4):
        b = (value // bit) % 2
        total = total + bit * ((1 - b) if k & bit else b)
    return total


def fill_weights(kern, forward, backward, layer):
    zero = jnp.zeros((3 * LANES, LANES), BF16)
    for ref in (forward, backward):
        ref[0 : 3 * LANES, LANES:] = zero
        ref[9 * LANES :, :LANES] = zero
    for p in range(3):
        for q in range(3):
            k = kern[layer, p, q]
            kt = k.T
            for u in range(2):
                a = ((p + u) * 3 + q) * LANES
                forward[a : a + LANES, u * LANES : (u + 1) * LANES] = k
                b = ((2 - p + u) * 3 + 2 - q) * LANES
                backward[b : b + LANES, u * LANES : (u + 1) * LANES] = kt


def windows(ref, row, s, left=0):
    out = []
    for t in range(4):
        for q in range(3):
            v = ref[pl.ds(row + t * s, s), left + q * s : left + q * s + T]
            out.append(v.reshape(s * T * 16, LANES))
    return jnp.concatenate(out, axis=1)


def stacked(ref, row, s, rows):
    return jnp.concatenate(
        [windows(ref, row + 2 * s * n, s) for n in range(rows // (2 * s))], axis=0
    )


def convolve(ref, weights, row, s, rows):
    both = jnp.dot(stacked(ref, row, s, rows), weights[...], preferred_element_type=F32)
    out = []
    m = T * 16
    for r in range(rows):
        n, u, e = r // (2 * s), (r // s) % 2, r % s
        at0 = (n * s + e) * m
        out.append(both[at0 : at0 + m, u * LANES : (u + 1) * LANES].reshape(T, 16, LANES))
    return out


def swap(low, n0, n1):
    return jnp.where(low, n0, pltpu.roll(n1, 4, 1)), jnp.where(low, pltpu.roll(n0, 4, 1), n1)


def low_half():
    return lax.broadcasted_iota(jnp.int32, (T // 2, 8, LANES), 1) < 4


def into_blocks(ref, c):
    low = low_half()
    n = [ref[CELL * c + e].astype(F32).reshape(T // 2, 8, LANES) for e in range(4)]
    lo = swap(low, n[0], n[1])
    hi = swap(low, n[2], n[3])
    both = [jnp.concatenate([lo[k], hi[k]], axis=1) for k in range(2)]
    return jnp.stack(both, axis=1).reshape(T, 16, LANES)


def out_of_blocks(ref, c, v):
    low = low_half()
    v = v.reshape(T // 2, 2, 16, LANES)
    for h in range(2):
        part = swap(low, v[:, 0, 8 * h : 8 * h + 8], v[:, 1, 8 * h : 8 * h + 8])
        for k in range(2):
            ref[CELL * c + 2 * h + k] = part[k].reshape(T * CELL, LANES).astype(ref.dtype)


def kernel(
    remote, f_hbm, g_hbm, kern, limit_ref, om_hbm, fg_hbm, res,
    fn, gn, f, a1, a1_rows, a1_cols, s1, a2, g2, g2_rows, g2_cols, g1, gf, w1, w1b, w2, w2b, rowm, colm, dw,
    full, got0, wxy, gxy, zbuf,
    local_sem, halo_send, halo_recv, ar_send, ar_recv,
):
    i, j, x, y, z, core = place()
    friends = [(lax.rem(i + dr + 16, 16), lax.rem(j + dc + 16, 16)) for dr, dc in SIDES]
    core_friend = at(x, y, z, 1 - core)
    z_friends = [at(x, y, flip(z, k), core) for k in range(1, 8)]
    xy = [(flip(x, k // 4), flip(y, k % 4)) for k in range(1, 16)]
    xy_friends = [at(a, b, z, core) for a, b in xy]
    if remote:
        barrier = pltpu.get_barrier_semaphore()
        everyone = friends + [core_friend] + z_friends + xy_friends
        for d in everyone:
            pl.semaphore_signal(barrier, inc=1, device_id=d, device_id_type=MESH)
    local = [
        pltpu.make_async_copy(f_hbm, fn, local_sem.at[0]),
        pltpu.make_async_copy(g_hbm, gn, local_sem.at[1]),
    ]
    for c in local:
        c.start()
    started = []

    def send(source, target, send_sem, recv_sem, device):
        c = pltpu.make_async_remote_copy(
            src_ref=source, dst_ref=target, send_sem=send_sem, recv_sem=recv_sem,
            device_id=device, device_id_type=MESH,
        )
        c.start()
        started.append(c)
        return c

    def exchange(n, ref, h):
        if not remote:
            return lambda: None
        src = {-1: pl.ds(h, h), 0: pl.ds(h, T), 1: pl.ds(T, h)}
        dst = {-1: pl.ds(h + T, h), 0: pl.ds(h, T), 1: pl.ds(0, h)}
        copies = [
            send(
                ref.at[src[dr], src[dc]], ref.at[dst[dr], dst[dc]],
                halo_send.at[n, m], halo_recv.at[n, m], friends[m],
            )
            for m, (dr, dc) in enumerate(SIDES)
        ]

        def finish():
            for c in copies:
                c.wait_recv()
            strips = [
                (i == 0, pl.ds(0, h), pl.ds(0, T + 2 * h)),
                (i == 15, pl.ds(T + h, h), pl.ds(0, T + 2 * h)),
                (j == 0, pl.ds(0, T + 2 * h), pl.ds(0, h)),
                (j == 15, pl.ds(0, T + 2 * h), pl.ds(T + h, h)),
            ]
            for edge, r, c in strips:

                @pl.when(edge)
                def _():
                    ref[r, c] = jnp.zeros((r.size, c.size, 16, LANES), BF16)

        return finish

    def strips(n, ref, h, rows, cols):
        for ref_part in (cols.at[:, pl.ds(0, h)], cols.at[:, pl.ds(T + h, h)]):
            ref_part[...] = jnp.zeros((2, h, h, 16, LANES), BF16)
        copies = []
        if remote:
            src = {-1: pl.ds(h, h), 0: pl.ds(h, T), 1: pl.ds(T, h)}
            dst = {-1: pl.ds(h + T, h), 0: pl.ds(h, T), 1: pl.ds(0, h)}
            for m, (dr, dc) in enumerate(SIDES):
                if dr:
                    target = rows.at[(1 - dr) // 2, pl.ds(0, h), dst[dc]]
                else:
                    target = cols.at[(1 - dc) // 2, dst[0]]
                copies.append(
                    send(
                        ref.at[src[dr], src[dc]], target,
                        halo_send.at[n, m], halo_recv.at[n, m], friends[m],
                    )
                )

        def finish():
            for c in copies:
                c.wait_recv()
            for k, edge in enumerate((0, 15)):

                @pl.when(i == edge)
                def _():
                    rows[k] = jnp.zeros((h, T + 2 * h, 16, LANES), BF16)

                @pl.when(j == edge)
                def _():
                    rows[:, :, k * (T + h) : k * (T + h) + h] = jnp.zeros(
                        (2, h, h, 16, LANES), BF16
                    )
                    cols[k] = jnp.zeros((T + 2 * h, h, 16, LANES), BF16)

            for k in range(2):
                lo = k * (T + h)
                ref[h : T + h, lo : lo + h] = cols[k, h : T + h]
                ref[lo : lo + h] = rows[k]

        return finish

    def borders(weights, h, rows, cols):
        def product(parts, taps):
            lhs = jnp.concatenate([v.reshape(h * T * 16, LANES) for v in parts], axis=1)
            rhs = jnp.concatenate(
                [weights[n * LANES : (n + 1) * LANES, :LANES] for n in taps], axis=0
            )
            return jnp.dot(lhs, rhs, preferred_element_type=F32)

        out = []
        for k in range(2):
            v = product(
                [rows[k, :, q * h : q * h + T] for q in range(3)],
                [2 * k * 3 + q for q in range(3)],
            )
            out.append((pl.ds(k * (T - h), h), pl.ds(0, T), v.reshape(h, T, 16, LANES)))
        for k in range(2):
            v = product(
                [cols[k, p * h : p * h + T] for p in range(3)],
                [p * 3 + 2 * k for p in range(3)],
            )
            out.append((pl.ds(0, T), pl.ds(k * (T - h), h), v.reshape(T, h, 16, LANES)))
        return out

    def zero_border(ref, h):
        ref[0:h] = jnp.zeros((h, T + 2 * h, 16, LANES), BF16)
        ref[T + h :] = jnp.zeros((h, T + 2 * h, 16, LANES), BF16)
        ref[:, 0:h] = jnp.zeros((T + 2 * h, h, 16, LANES), BF16)
        ref[:, T + h :] = jnp.zeros((T + 2 * h, h, 16, LANES), BF16)

    def live(r, c):
        return rowm[r][:, None] * colm[c][None]

    def shifted(d, n):
        return pl.ds(d.start + n, d.size)

    limit = limit_ref[0]
    sub = lax.broadcasted_iota(jnp.int32, (T, 16, LANES), 1)
    blk = lax.broadcasted_iota(jnp.int32, (T, 16, LANES), 0) * CELL
    rowm[...] = jnp.where(blk + sub // CELL + i * (T * CELL) < limit, 1.0, 0.0).astype(F32)
    colm[...] = jnp.where(blk + sub % CELL + j * (T * CELL) < limit, 1.0, 0.0).astype(F32)
    own1, own2 = pl.ds(ONE, T), pl.ds(TWO, T)

    def prepare_f(c, _):
        v = into_blocks(fn, c)
        f[c] = v.astype(BF16)
        a1[c + ONE, own1] = (elu(v) * (rowm[c] * colm[...])).astype(BF16)
        return 0

    def prepare_g(c, _):
        v = into_blocks(gn, c)
        g2[c + TWO, own2] = (v * (rowm[c] * colm[...])).astype(BF16)
        return 0

    zero_border(a1, ONE)
    zero_border(g2, TWO)
    local[0].wait()
    lax.fori_loop(0, T, prepare_f, 0)
    local[1].wait()
    lax.fori_loop(0, T, prepare_g, 0)
    if remote:
        pl.semaphore_wait(barrier, len(everyone))
    finish_a1 = strips(0, a1, ONE, a1_rows, a1_cols)
    finish_g2 = strips(1, g2, TWO, g2_rows, g2_cols)
    fill_weights(kern, w1, w1b, 0)
    fill_weights(kern, w2, w2b, 1)

    def conv1(k, _):
        for e, v in enumerate(convolve(a1, w1, k * R, ONE, R)):
            r = k * R + e
            v = v + f[r].astype(F32)
            s1[r] = v
            a2[r + TWO, own2] = (elu(v) * (rowm[r] * colm[...])).astype(BF16)
        return 0

    lax.fori_loop(0, T // R, conv1, 0)
    finish_a1()
    edges = borders(w1, ONE, a1_rows, a1_cols)
    for r, c, v in edges:
        s1[r, c] += v
    for r, c, _ in edges:
        a2[shifted(r, TWO), shifted(c, TWO)] = (elu(s1[r, c]) * live(r, c)).astype(BF16)
    finish_a2 = exchange(2, a2, TWO)

    def contract(own, o, wide, s, layer, turned):
        lhs = []
        for n in range(T // (2 * s)):
            b = 2 * s * n
            gs = [
                own[pl.ds(b + o + u * s, s), o : o + T].reshape(s * T * 16, LANES)
                for u in range(2)
            ]
            lhs.append(jnp.concatenate(gs, axis=1))
        lhs = jnp.concatenate(lhs, axis=0)
        rhs = stacked(wide, 0, s, T)
        dw[...] = lax.dot_general(lhs, rhs, (((0,), (0,)), ((), ())), preferred_element_type=F32)
        for p in range(3):
            for q in range(3):
                a, b = (p, q) if turned else (2 - p, 2 - q)
                lo = (a * 3 + b) * LANES
                hi = ((a + 1) * 3 + b) * LANES
                v = dw[:LANES, lo : lo + LANES] + dw[LANES:, hi : hi + LANES]
                v = (v.T if turned else v).reshape(2, 8, 8, LANES)
                for h in range(2):
                    n = (p * 3 + q) * 16 + 8 * h
                    full[layer, n // HALF, n % HALF : n % HALF + 8] = v[h]
        full[layer, :, HALF:] = jnp.zeros((2, PADDED - HALF, 8, LANES), F32)

    mine = x * 4 + y
    mine_at = pl.ds(mine * PIECE, PIECE)

    class Reduction:
        def __init__(self, layer):
            self.layer, self.slot, self.pending = layer, 0, []

        def send(self, source, target, device):
            n = self.slot
            self.slot += 1
            sems = ar_send.at[self.layer, n], ar_recv.at[self.layer, n]
            self.pending.append(send(source, target, *sems, device))

        def arrive(self):
            for c in self.pending:
                c.wait_recv()
            self.pending = []

        def core_out(self):
            n = self.layer
            if remote:
                self.send(full.at[n, 1 - core], got0.at[n], core_friend)

        def plane_out(self):
            n = self.layer
            if not remote:
                return
            self.arrive()
            v = full[n, core] + got0[n]
            full[n, core] = v
            wxy[n] = v.reshape(16, PIECE, 8, LANES).astype(WIRE)
            for k, (a, b) in enumerate(xy):
                self.send(wxy.at[n, a * 4 + b], gxy.at[n, k], xy_friends[k])

        def z_out(self):
            n = self.layer
            if not remote:
                return
            self.arrive()
            v = full[n, core, mine_at]
            for k in range(15):
                v = v + gxy[n, k].astype(F32)
            zbuf[n, z] = v.astype(WIRE)
            for d in z_friends:
                self.send(zbuf.at[n, z], zbuf.at[n, z], d)

        def plane_back(self):
            n = self.layer
            if not remote:
                return
            self.arrive()
            v = zbuf[n, 0].astype(F32)
            for k in range(1, 8):
                v = v + zbuf[n, k].astype(F32)
            res[n, core, mine_at] = (v / limit.astype(F32)).astype(WIRE)
            piece = res.at[n, core, mine_at]
            for d in xy_friends:
                self.send(piece, piece, d)
            self.coming, self.pending = self.pending, []
            self.send(piece, piece, core_friend)

        def core_back(self):
            n = self.layer
            if not remote:
                res[n] = (full[n] / limit.astype(F32)).astype(WIRE)
                return
            for k in sorted(range(15), key=lambda k: HOPS[k]):
                self.coming[k].wait_recv()
                a, b = xy[k]
                piece = res.at[n, core, pl.ds((a * 4 + b) * PIECE, PIECE)]
                self.send(piece, piece, core_friend)

    second, first = Reduction(1), Reduction(0)

    def back2(k, _):
        for e, v in enumerate(convolve(g2, w2b, k * R, TWO, R)):
            r = k * R + e
            m = rowm[r] * colm[...]
            v = g2[r + TWO, own2].astype(F32) + m * slope(s1[r]) * v
            gf[r] = v
            g1[r + ONE, own1] = v.astype(BF16)
        return 0

    lax.fori_loop(0, T // R, back2, 0)
    finish_g2()
    edges = borders(w2b, TWO, g2_rows, g2_cols)
    for r, c, v in edges:
        gf[r, c] += live(r, c) * slope(s1[r, c]) * v
    for r, c, _ in edges:
        g1[shifted(r, ONE), shifted(c, ONE)] = gf[r, c].astype(BF16)
    finish_g1 = exchange(3, g1, ONE)
    contract(a2, TWO, g2, TWO, 1, False)
    second.core_out()
    contract(g1, ONE, a1, ONE, 0, True)
    first.core_out()
    second.plane_out()

    def conv2(k, _):
        for e, v in enumerate(convolve(a2, w2, k * R, TWO, R)):
            r = k * R + e
            out_of_blocks(fn, r, rowm[r] * colm[...] * (s1[r] + v))
        return 0

    finish_a2()
    lax.fori_loop(0, T // R // 2, conv2, 0)
    first.plane_out()
    lax.fori_loop(T // R // 2, T // R, conv2, 0)
    om = pltpu.make_async_copy(fn, om_hbm, local_sem.at[2])
    om.start()

    def back1(k, _):
        for e, v in enumerate(convolve(g1, w1b, k * R, ONE, R)):
            r = k * R + e
            m = rowm[r] * colm[...]
            out_of_blocks(gn, r, gf[r] + m * slope(f[r].astype(F32)) * v)
        return 0

    finish_g1()
    lax.fori_loop(0, T // R // 2, back1, 0)
    second.z_out()
    lax.fori_loop(T // R // 2, T // R, back1, 0)
    fg = pltpu.make_async_copy(gn, fg_hbm, local_sem.at[3])
    fg.start()
    first.z_out()
    second.plane_back()
    first.plane_back()
    second.core_back()
    first.core_back()
    om.wait()
    fg.wait()
    second.arrive()
    first.arrive()
    for c in started:
        c.wait_send()


R = 8


def call(remote, f, g, kernels, length):
    vm = pltpu.VMEM
    sems = pltpu.SemaphoreType.DMA
    tile = (T * CELL, T * CELL, LANES)

    def blocks(h, kind):
        return vm((T + 2 * h, T + 2 * h, 16, LANES), kind)

    return pl.pallas_call(
        functools.partial(kernel, remote),
        out_shape=(
            jax.ShapeDtypeStruct(tile, BF16),
            jax.ShapeDtypeStruct(tile, BF16),
            jax.ShapeDtypeStruct((2, 2, PADDED, 8, LANES), WIRE),
        ),
        in_specs=[
            pl.BlockSpec(memory_space=pl.ANY),
            pl.BlockSpec(memory_space=pl.ANY),
            pl.BlockSpec(memory_space=pltpu.VMEM),
            pl.BlockSpec(memory_space=pltpu.SMEM),
        ],
        out_specs=[
            pl.BlockSpec(memory_space=pl.ANY),
            pl.BlockSpec(memory_space=pl.ANY),
            pl.BlockSpec(memory_space=pltpu.VMEM),
        ],
        scratch_shapes=[
            vm(tile, BF16),
            vm(tile, BF16),
            blocks(0, BF16),
            blocks(ONE, BF16),
            vm((2, ONE, T + 2 * ONE, 16, LANES), BF16),
            vm((2, T + 2 * ONE, ONE, 16, LANES), BF16),
            blocks(0, F32),
            blocks(TWO, BF16),
            blocks(TWO, BF16),
            vm((2, TWO, T + 2 * TWO, 16, LANES), BF16),
            vm((2, T + 2 * TWO, TWO, 16, LANES), BF16),
            blocks(ONE, BF16),
            blocks(0, F32),
            vm((12 * LANES, 2 * LANES), BF16),
            vm((12 * LANES, 2 * LANES), BF16),
            vm((12 * LANES, 2 * LANES), BF16),
            vm((12 * LANES, 2 * LANES), BF16),
            vm((T, 16, LANES), F32),
            vm((T, 16, LANES), F32),
            vm((2 * LANES, 12 * LANES), F32),
            vm((2, 2, PADDED, 8, LANES), F32),
            vm((2, PADDED, 8, LANES), F32),
            vm((2, 16, PIECE, 8, LANES), WIRE),
            vm((2, 15, PIECE, 8, LANES), WIRE),
            vm((2, 8, PIECE, 8, LANES), WIRE),
            sems((4,)),
            sems((4, 8)),
            sems((4, 8)),
            sems((2, 54)),
            sems((2, 54)),
        ],
        compiler_params=pltpu.CompilerParams(
            collective_id=0 if remote else None, has_side_effects=True, vmem_limit_bytes=60 << 20
        ),
    )(f, g, kernels, length)


def place_kernel(om_in, fg_in, kg_in, om_out, fg_out, kg_out, a, b, k, wide, sems):
    half = T * CELL // 2
    moves = [(kg_in, k, None)]
    for source, held, target in ((om_in, a, om_out), (fg_in, b, fg_out)):
        for n in range(2):
            d = pl.ds(n * half, half)
            moves.append((source.at[d], held.at[d], target.at[d]))
    ins = [
        pltpu.make_async_copy(source, held, sems.at[0, n])
        for n, (source, held, _) in enumerate(moves)
    ]
    for c in ins:
        c.start()
    outs = []
    for n, (_, held, target) in enumerate(moves):
        ins[n].wait()
        if target is None:
            wide[...] = k[:, :, :HALF].astype(F32)
            held, target = wide, kg_out
        c = pltpu.make_async_copy(held, target, sems.at[1, n])
        c.start()
        outs.append(c)
    for c in outs:
        c.wait()


def body(features, kernels, length, cotangent):
    om, fg, kg = call(True, features, cotangent, kernels, length)
    vm = pltpu.VMEM
    om, fg, kg = pl.pallas_call(
        place_kernel,
        out_shape=(
            jax.ShapeDtypeStruct(om.shape, om.dtype),
            jax.ShapeDtypeStruct(fg.shape, fg.dtype),
            jax.ShapeDtypeStruct((2, 2, HALF, 8, LANES), F32),
        ),
        in_specs=[pl.BlockSpec(memory_space=pl.ANY)] * 3,
        out_specs=[pl.BlockSpec(memory_space=pl.ANY)] * 3,
        scratch_shapes=[
            vm(om.shape, om.dtype),
            vm(fg.shape, fg.dtype),
            vm(kg.shape, kg.dtype),
            vm((2, 2, HALF, 8, LANES), F32),
            pltpu.SemaphoreType.DMA((2, 5)),
        ],
    )(om, fg, kg)
    return om, fg, kg.reshape(kernels.shape)


def solution(mesh):
    in_specs = (P("row", "col", None), P(), P(), P("row", "col", None))
    out_specs = (P("row", "col", None), P("row", "col", None), P())
    return jax.shard_map(body, mesh=mesh, in_specs=in_specs, out_specs=out_specs, check_vma=False)
```

```python
import functools

import jax
import jax.numpy as jnp
from jax import lax
from jax.experimental import pallas as pl
from jax.experimental.pallas import tpu as pltpu
from jax.sharding import PartitionSpec as P

MESH = pl.DeviceIdType.MESH
F32, BF16 = jnp.float32, jnp.bfloat16
FIRST_SPACING = 4
SECOND_SPACING = 8
CELL = 4
ONE, TWO = FIRST_SPACING // CELL, SECOND_SPACING // CELL
T = 16
LANES = 128
SIDES = [(r, c) for r in (-1, 0, 1) for c in (-1, 0, 1) if (r, c) != (0, 0)]
HALF = 72
PIECE = 5
PADDED = 16 * PIECE
WIRE = BF16
HOPS = [(0, 1, 2, 1)[k // 4] + (0, 1, 2, 1)[k % 4] for k in range(1, 16)]


def exp_low(values):
    return jnp.exp(jnp.minimum(values, 0.0))


def elu(values):
    return jnp.where(values > 0, values, exp_low(values) - 1.0)


def slope(values):
    return jnp.where(values > 0, 1.0, exp_low(values))


def place():
    i, j = lax.axis_index("row"), lax.axis_index("col")
    x_lo, z = i // 8, i % 8
    y, x_hi, core = j // 4, (j // 2) % 2, j % 2
    return i, j, x_hi * 2 + x_lo, y, z, core


def at(x, y, z, core):
    return ((x % 2) * 8 + z, y * 4 + (x // 2) * 2 + core)


def flip(value, k):
    total = 0
    for bit in (1, 2, 4):
        b = (value // bit) % 2
        total = total + bit * ((1 - b) if k & bit else b)
    return total


def fill_weights(kern, forward, backward, layer):
    zero = jnp.zeros((3 * LANES, LANES), BF16)
    for ref in (forward, backward):
        ref[0 : 3 * LANES, LANES:] = zero
        ref[9 * LANES :, :LANES] = zero
    for p in range(3):
        for q in range(3):
            k = kern[layer, p, q]
            kt = k.T
            for u in range(2):
                a = ((p + u) * 3 + q) * LANES
                forward[a : a + LANES, u * LANES : (u + 1) * LANES] = k
                b = ((2 - p + u) * 3 + 2 - q) * LANES
                backward[b : b + LANES, u * LANES : (u + 1) * LANES] = kt


def windows(ref, row, s, left=0):
    out = []
    for t in range(4):
        for q in range(3):
            v = ref[pl.ds(row + t * s, s), left + q * s : left + q * s + T]
            out.append(v.reshape(s * T * 16, LANES))
    return jnp.concatenate(out, axis=1)


def stacked(ref, row, s, rows):
    return jnp.concatenate(
        [windows(ref, row + 2 * s * n, s) for n in range(rows // (2 * s))], axis=0
    )


def convolve(ref, weights, row, s, rows):
    both = jnp.dot(stacked(ref, row, s, rows), weights[...], preferred_element_type=F32)
    out = []
    m = T * 16
    for r in range(rows):
        n, u, e = r // (2 * s), (r // s) % 2, r % s
        at0 = (n * s + e) * m
        out.append(both[at0 : at0 + m, u * LANES : (u + 1) * LANES].reshape(T, 16, LANES))
    return out


def swap(low, n0, n1):
    return jnp.where(low, n0, pltpu.roll(n1, 4, 1)), jnp.where(low, pltpu.roll(n0, 4, 1), n1)


def low_half():
    return lax.broadcasted_iota(jnp.int32, (T // 2, 8, LANES), 1) < 4


def into_blocks(ref, c):
    low = low_half()
    n = [ref[CELL * c + e].astype(F32).reshape(T // 2, 8, LANES) for e in range(4)]
    lo = swap(low, n[0], n[1])
    hi = swap(low, n[2], n[3])
    both = [jnp.concatenate([lo[k], hi[k]], axis=1) for k in range(2)]
    return jnp.stack(both, axis=1).reshape(T, 16, LANES)


def out_of_blocks(ref, c, v):
    low = low_half()
    v = v.reshape(T // 2, 2, 16, LANES)
    for h in range(2):
        part = swap(low, v[:, 0, 8 * h : 8 * h + 8], v[:, 1, 8 * h : 8 * h + 8])
        for k in range(2):
            ref[CELL * c + 2 * h + k] = part[k].reshape(T * CELL, LANES).astype(ref.dtype)


def kernel(
    remote, f_hbm, g_hbm, kern, limit_ref, om_hbm, fg_hbm, res,
    fn, gn, f, a1, a1_rows, a1_cols, s1, a2, g2, g2_rows, g2_cols, g1, gf, w1, w1b, w2, w2b, rowm, colm, dw,
    full, got0, wxy, gxy, zbuf,
    local_sem, halo_send, halo_recv, ar_send, ar_recv,
):
    i, j, x, y, z, core = place()
    def inside(dr, dc):
        return (i + dr >= 0) & (i + dr < 16) & (j + dc >= 0) & (j + dc < 16)

    friends = [(lax.rem(i + dr + 16, 16), lax.rem(j + dc + 16, 16)) for dr, dc in SIDES]
    core_friend = at(x, y, z, 1 - core)
    z_friends = [at(x, y, flip(z, k), core) for k in range(1, 8)]
    xy = [(flip(x, k // 4), flip(y, k % 4)) for k in range(1, 16)]
    xy_friends = [at(a, b, z, core) for a, b in xy]
    if remote:
        barrier = pltpu.get_barrier_semaphore()
        everyone = friends + [core_friend] + z_friends + xy_friends
        for d in everyone:
            pl.semaphore_signal(barrier, inc=1, device_id=d, device_id_type=MESH)
    local = [
        pltpu.make_async_copy(f_hbm, fn, local_sem.at[0]),
        pltpu.make_async_copy(g_hbm, gn, local_sem.at[1]),
    ]
    for c in local:
        c.start()
    started = []

    def send(source, target, send_sem, recv_sem, device, go=None):
        c = pltpu.make_async_remote_copy(
            src_ref=source, dst_ref=target, send_sem=send_sem, recv_sem=recv_sem,
            device_id=device, device_id_type=MESH,
        )
        if go is None:
            c.start()
        else:
            pl.when(go)(c.start)
        started.append((c, go))
        return c

    def exchange(n, ref, h):
        if not remote:
            return lambda: None
        src = {-1: pl.ds(h, h), 0: pl.ds(h, T), 1: pl.ds(T, h)}
        dst = {-1: pl.ds(h + T, h), 0: pl.ds(h, T), 1: pl.ds(0, h)}
        copies = [
            send(
                ref.at[src[dr], src[dc]], ref.at[dst[dr], dst[dc]],
                halo_send.at[n, m], halo_recv.at[n, m], friends[m], inside(dr, dc),
            )
            for m, (dr, dc) in enumerate(SIDES)
        ]

        def finish():
            for c, (dr, dc) in zip(copies, SIDES):
                pl.when(inside(-dr, -dc))(c.wait_recv)
            strips = [
                (i == 0, pl.ds(0, h), pl.ds(0, T + 2 * h)),
                (i == 15, pl.ds(T + h, h), pl.ds(0, T + 2 * h)),
                (j == 0, pl.ds(0, T + 2 * h), pl.ds(0, h)),
                (j == 15, pl.ds(0, T + 2 * h), pl.ds(T + h, h)),
            ]
            for edge, r, c in strips:

                @pl.when(edge)
                def _():
                    ref[r, c] = jnp.zeros((r.size, c.size, 16, LANES), BF16)

        return finish

    def strips(n, ref, h, rows, cols):
        for ref_part in (cols.at[:, pl.ds(0, h)], cols.at[:, pl.ds(T + h, h)]):
            ref_part[...] = jnp.zeros((2, h, h, 16, LANES), BF16)
        copies = []
        if remote:
            src = {-1: pl.ds(h, h), 0: pl.ds(h, T), 1: pl.ds(T, h)}
            dst = {-1: pl.ds(h + T, h), 0: pl.ds(h, T), 1: pl.ds(0, h)}
            for m, (dr, dc) in enumerate(SIDES):
                if dr:
                    target = rows.at[(1 - dr) // 2, pl.ds(0, h), dst[dc]]
                else:
                    target = cols.at[(1 - dc) // 2, dst[0]]
                copies.append(
                    send(
                        ref.at[src[dr], src[dc]], target,
                        halo_send.at[n, m], halo_recv.at[n, m], friends[m], inside(dr, dc),
                    )
                )

        def finish():
            for c, (dr, dc) in zip(copies, SIDES):
                pl.when(inside(-dr, -dc))(c.wait_recv)
            for k, edge in enumerate((0, 15)):

                @pl.when(i == edge)
                def _():
                    rows[k] = jnp.zeros((h, T + 2 * h, 16, LANES), BF16)

                @pl.when(j == edge)
                def _():
                    rows[:, :, k * (T + h) : k * (T + h) + h] = jnp.zeros(
                        (2, h, h, 16, LANES), BF16
                    )
                    cols[k] = jnp.zeros((T + 2 * h, h, 16, LANES), BF16)

            for k in range(2):
                lo = k * (T + h)
                ref[h : T + h, lo : lo + h] = cols[k, h : T + h]
                ref[lo : lo + h] = rows[k]

        return finish

    def borders(weights, h, rows, cols):
        def product(parts, taps):
            lhs = jnp.concatenate([v.reshape(h * T * 16, LANES) for v in parts], axis=1)
            rhs = jnp.concatenate(
                [weights[n * LANES : (n + 1) * LANES, :LANES] for n in taps], axis=0
            )
            return jnp.dot(lhs, rhs, preferred_element_type=F32)

        out = []
        for k in range(2):
            v = product(
                [rows[k, :, q * h : q * h + T] for q in range(3)],
                [2 * k * 3 + q for q in range(3)],
            )
            out.append((pl.ds(k * (T - h), h), pl.ds(0, T), v.reshape(h, T, 16, LANES)))
        for k in range(2):
            v = product(
                [cols[k, p * h : p * h + T] for p in range(3)],
                [p * 3 + 2 * k for p in range(3)],
            )
            out.append((pl.ds(0, T), pl.ds(k * (T - h), h), v.reshape(T, h, 16, LANES)))
        return out

    def zero_border(ref, h):
        ref[0:h] = jnp.zeros((h, T + 2 * h, 16, LANES), BF16)
        ref[T + h :] = jnp.zeros((h, T + 2 * h, 16, LANES), BF16)
        ref[:, 0:h] = jnp.zeros((T + 2 * h, h, 16, LANES), BF16)
        ref[:, T + h :] = jnp.zeros((T + 2 * h, h, 16, LANES), BF16)

    def live(r, c):
        return rowm[r][:, None] * colm[c][None]

    def shifted(d, n):
        return pl.ds(d.start + n, d.size)

    limit = limit_ref[0]
    sub = lax.broadcasted_iota(jnp.int32, (T, 16, LANES), 1)
    blk = lax.broadcasted_iota(jnp.int32, (T, 16, LANES), 0) * CELL
    rowm[...] = jnp.where(blk + sub // CELL + i * (T * CELL) < limit, 1.0, 0.0).astype(F32)
    colm[...] = jnp.where(blk + sub % CELL + j * (T * CELL) < limit, 1.0, 0.0).astype(F32)
    own1, own2 = pl.ds(ONE, T), pl.ds(TWO, T)

    def prepare_f(c, _):
        v = into_blocks(fn, c)
        f[c] = v.astype(BF16)
        a1[c + ONE, own1] = (elu(v) * (rowm[c] * colm[...])).astype(BF16)
        return 0

    def prepare_g(c, _):
        v = into_blocks(gn, c)
        g2[c + TWO, own2] = (v * (rowm[c] * colm[...])).astype(BF16)
        return 0

    zero_border(a1, ONE)
    zero_border(g2, TWO)
    local[0].wait()
    lax.fori_loop(0, T, prepare_f, 0)
    local[1].wait()
    lax.fori_loop(0, T, prepare_g, 0)
    if remote:
        pl.semaphore_wait(barrier, len(everyone))
    finish_a1 = strips(0, a1, ONE, a1_rows, a1_cols)
    finish_g2 = strips(1, g2, TWO, g2_rows, g2_cols)
    fill_weights(kern, w1, w1b, 0)
    fill_weights(kern, w2, w2b, 1)

    def conv1(k, _):
        for e, v in enumerate(convolve(a1, w1, k * R, ONE, R)):
            r = k * R + e
            v = v + f[r].astype(F32)
            s1[r] = v
            a2[r + TWO, own2] = (elu(v) * (rowm[r] * colm[...])).astype(BF16)
        return 0

    lax.fori_loop(0, T // R, conv1, 0)
    finish_a1()
    edges = borders(w1, ONE, a1_rows, a1_cols)
    for r, c, v in edges:
        s1[r, c] += v
    for r, c, _ in edges:
        a2[shifted(r, TWO), shifted(c, TWO)] = (elu(s1[r, c]) * live(r, c)).astype(BF16)

    def contract(own, o, wide, s, layer, turned):
        lhs = []
        for n in range(T // (2 * s)):
            b = 2 * s * n
            gs = [
                own[pl.ds(b + o + u * s, s), o : o + T].reshape(s * T * 16, LANES)
                for u in range(2)
            ]
            lhs.append(jnp.concatenate(gs, axis=1))
        lhs = jnp.concatenate(lhs, axis=0)
        rhs = stacked(wide, 0, s, T)
        dw[...] = lax.dot_general(lhs, rhs, (((0,), (0,)), ((), ())), preferred_element_type=F32)
        for p in range(3):
            for q in range(3):
                a, b = (p, q) if turned else (2 - p, 2 - q)
                lo = (a * 3 + b) * LANES
                hi = ((a + 1) * 3 + b) * LANES
                v = dw[:LANES, lo : lo + LANES] + dw[LANES:, hi : hi + LANES]
                v = (v.T if turned else v).reshape(2, 8, 8, LANES)
                for h in range(2):
                    n = (p * 3 + q) * 16 + 8 * h
                    full[layer, n // HALF, n % HALF : n % HALF + 8] = v[h]
        full[layer, :, HALF:] = jnp.zeros((2, PADDED - HALF, 8, LANES), F32)

    mine = x * 4 + y
    mine_at = pl.ds(mine * PIECE, PIECE)

    class Reduction:
        def __init__(self, layer):
            self.layer, self.slot, self.pending = layer, 0, []

        def send(self, source, target, device):
            n = self.slot
            self.slot += 1
            sems = ar_send.at[self.layer, n], ar_recv.at[self.layer, n]
            self.pending.append(send(source, target, *sems, device))

        def arrive(self):
            for c in self.pending:
                c.wait_recv()
            self.pending = []

        def core_out(self):
            n = self.layer
            if remote:
                self.send(full.at[n, 1 - core], got0.at[n], core_friend)

        def plane_out(self):
            n = self.layer
            if not remote:
                return
            self.arrive()
            v = full[n, core] + got0[n]
            full[n, core] = v
            wxy[n] = v.reshape(16, PIECE, 8, LANES).astype(WIRE)
            for k, (a, b) in enumerate(xy):
                self.send(wxy.at[n, a * 4 + b], gxy.at[n, k], xy_friends[k])

        def z_out(self):
            n = self.layer
            if not remote:
                return
            self.arrive()
            v = full[n, core, mine_at]
            for k in range(15):
                v = v + gxy[n, k].astype(F32)
            zbuf[n, z] = v.astype(WIRE)
            for d in z_friends:
                self.send(zbuf.at[n, z], zbuf.at[n, z], d)

        def plane_back(self):
            n = self.layer
            if not remote:
                return
            self.arrive()
            v = zbuf[n, 0].astype(F32)
            for k in range(1, 8):
                v = v + zbuf[n, k].astype(F32)
            res[n, core, mine_at] = (v / limit.astype(F32)).astype(WIRE)
            piece = res.at[n, core, mine_at]
            for d in xy_friends:
                self.send(piece, piece, d)
            self.coming, self.pending = self.pending, []
            self.send(piece, piece, core_friend)

        def core_back(self):
            n = self.layer
            if not remote:
                res[n] = (full[n] / limit.astype(F32)).astype(WIRE)
                return
            for k in sorted(range(15), key=lambda k: HOPS[k]):
                self.coming[k].wait_recv()
                a, b = xy[k]
                piece = res.at[n, core, pl.ds((a * 4 + b) * PIECE, PIECE)]
                self.send(piece, piece, core_friend)

    second, first = Reduction(1), Reduction(0)

    def back2(k, _):
        for e, v in enumerate(convolve(g2, w2b, k * R, TWO, R)):
            r = k * R + e
            m = rowm[r] * colm[...]
            v = g2[r + TWO, own2].astype(F32) + m * slope(s1[r]) * v
            gf[r] = v
            g1[r + ONE, own1] = v.astype(BF16)
        return 0

    lax.fori_loop(0, T // R, back2, 0)
    finish_g2()
    edges = borders(w2b, TWO, g2_rows, g2_cols)
    for r, c, v in edges:
        gf[r, c] += live(r, c) * slope(s1[r, c]) * v
    for r, c, _ in edges:
        g1[shifted(r, ONE), shifted(c, ONE)] = gf[r, c].astype(BF16)
    finish_g1 = exchange(3, g1, ONE)
    contract(a2, TWO, g2, TWO, 1, False)
    second.core_out()
    contract(g1, ONE, a1, ONE, 0, True)
    first.core_out()
    second.plane_out()

    def conv2(k, _):
        for e, v in enumerate(convolve(a2, w2, k * R, TWO, R)):
            r = k * R + e
            out_of_blocks(fn, r, rowm[r] * colm[...] * (s1[r] + v))
        return 0

    def back1(k, _):
        for e, v in enumerate(convolve(g1, w1b, k * R, ONE, R)):
            r = k * R + e
            m = rowm[r] * colm[...]
            out_of_blocks(gn, r, gf[r] + m * slope(f[r].astype(F32)) * v)
        return 0

    first.plane_out()
    finish_a2 = exchange(2, a2, TWO)
    second.z_out()
    first.z_out()
    finish_g1()
    lax.fori_loop(0, T // R, back1, 0)
    fg = pltpu.make_async_copy(gn, fg_hbm, local_sem.at[3])
    fg.start()
    second.plane_back()
    first.plane_back()
    finish_a2()
    lax.fori_loop(0, T // R, conv2, 0)
    om = pltpu.make_async_copy(fn, om_hbm, local_sem.at[2])
    om.start()
    second.core_back()
    first.core_back()
    om.wait()
    fg.wait()
    second.arrive()
    first.arrive()
    for c, go in started:
        if go is None:
            c.wait_send()
        else:
            pl.when(go)(c.wait_send)


R = 8


def call(remote, f, g, kernels, length):
    vm = pltpu.VMEM
    sems = pltpu.SemaphoreType.DMA
    tile = (T * CELL, T * CELL, LANES)

    def blocks(h, kind):
        return vm((T + 2 * h, T + 2 * h, 16, LANES), kind)

    return pl.pallas_call(
        functools.partial(kernel, remote),
        out_shape=(
            jax.ShapeDtypeStruct(tile, BF16),
            jax.ShapeDtypeStruct(tile, BF16),
            jax.ShapeDtypeStruct((2, 2, PADDED, 8, LANES), WIRE),
        ),
        in_specs=[
            pl.BlockSpec(memory_space=pltpu.HBM),
            pl.BlockSpec(memory_space=pltpu.HBM),
            pl.BlockSpec(memory_space=pltpu.VMEM),
            pl.BlockSpec(memory_space=pltpu.SMEM),
        ],
        out_specs=[
            pl.BlockSpec(memory_space=pl.ANY),
            pl.BlockSpec(memory_space=pl.ANY),
            pl.BlockSpec(memory_space=pltpu.VMEM),
        ],
        scratch_shapes=[
            vm(tile, BF16),
            vm(tile, BF16),
            blocks(0, BF16),
            blocks(ONE, BF16),
            vm((2, ONE, T + 2 * ONE, 16, LANES), BF16),
            vm((2, T + 2 * ONE, ONE, 16, LANES), BF16),
            blocks(0, F32),
            blocks(TWO, BF16),
            blocks(TWO, BF16),
            vm((2, TWO, T + 2 * TWO, 16, LANES), BF16),
            vm((2, T + 2 * TWO, TWO, 16, LANES), BF16),
            blocks(ONE, BF16),
            blocks(0, F32),
            vm((12 * LANES, 2 * LANES), BF16),
            vm((12 * LANES, 2 * LANES), BF16),
            vm((12 * LANES, 2 * LANES), BF16),
            vm((12 * LANES, 2 * LANES), BF16),
            vm((T, 16, LANES), F32),
            vm((T, 16, LANES), F32),
            vm((2 * LANES, 12 * LANES), F32),
            vm((2, 2, PADDED, 8, LANES), F32),
            vm((2, PADDED, 8, LANES), F32),
            vm((2, 16, PIECE, 8, LANES), WIRE),
            vm((2, 15, PIECE, 8, LANES), WIRE),
            vm((2, 8, PIECE, 8, LANES), WIRE),
            sems((4,)),
            sems((4, 8)),
            sems((4, 8)),
            sems((2, 54)),
            sems((2, 54)),
        ],
        compiler_params=pltpu.CompilerParams(
            collective_id=0 if remote else None, has_side_effects=True, vmem_limit_bytes=50 << 20
        ),
    )(f, g, kernels, length)


def place_kernel(om_in, fg_in, kg_in, om_out, fg_out, kg_out, k, wide, sems):
    moves = [(kg_in, k), (om_in, om_out), (fg_in, fg_out)]
    copies = [
        pltpu.make_async_copy(source, target, sems.at[n])
        for n, (source, target) in enumerate(moves)
    ]
    for c in copies:
        c.start()
    copies[0].wait()
    wide[...] = k[:, :, :HALF].astype(F32)
    last = pltpu.make_async_copy(wide, kg_out, sems.at[3])
    last.start()
    for c in copies[1:]:
        c.wait()
    last.wait()


def body(features, kernels, length, cotangent):
    om, fg, kg = call(True, features, cotangent, kernels, length)
    vm = pltpu.VMEM
    om, fg, kg = pl.pallas_call(
        place_kernel,
        out_shape=(
            jax.ShapeDtypeStruct(om.shape, om.dtype),
            jax.ShapeDtypeStruct(fg.shape, fg.dtype),
            jax.ShapeDtypeStruct((2, 2, HALF, 8, LANES), F32),
        ),
        in_specs=[pl.BlockSpec(memory_space=pl.ANY)] * 3,
        out_specs=[pl.BlockSpec(memory_space=pl.ANY)] * 3,
        scratch_shapes=[
            vm(kg.shape, kg.dtype),
            vm((2, 2, HALF, 8, LANES), F32),
            pltpu.SemaphoreType.DMA((4,)),
        ],
        compiler_params=pltpu.CompilerParams(vmem_limit_bytes=8 << 20),
    )(om, fg, kg)
    return om, fg, kg.reshape(kernels.shape)


def solution(mesh):
    in_specs = (P("row", "col", None), P(), P(), P("row", "col", None))
    out_specs = (P("row", "col", None), P("row", "col", None), P())
    return jax.shard_map(body, mesh=mesh, in_specs=in_specs, out_specs=out_specs, check_vma=False)
```

```python
import functools

import jax
import jax.numpy as jnp
from jax import lax
from jax.experimental import pallas as pl
from jax.experimental.pallas import tpu as pltpu
from jax.sharding import PartitionSpec as P

MESH = pl.DeviceIdType.MESH
F32, BF16 = jnp.float32, jnp.bfloat16
FIRST_SPACING = 4
SECOND_SPACING = 8
CELL = 4
ONE, TWO = FIRST_SPACING // CELL, SECOND_SPACING // CELL
T = 16
LANES = 128
SIDES = [(r, c) for r in (-1, 0, 1) for c in (-1, 0, 1) if (r, c) != (0, 0)]
HALF = 72
PIECE = 5
PADDED = 16 * PIECE
WIRE = BF16
HOPS = [(0, 1, 2, 1)[k // 4] + (0, 1, 2, 1)[k % 4] for k in range(1, 16)]
FAR_FIRST = sorted(range(15), key=lambda k: -HOPS[k])


def exp_low(values):
    return jnp.exp(jnp.minimum(values, 0.0))


def elu(values):
    return jnp.where(values > 0, values, exp_low(values) - 1.0)


def slope(values):
    return jnp.where(values > 0, 1.0, exp_low(values))


def place():
    i, j = lax.axis_index("row"), lax.axis_index("col")
    x_lo, z = i // 8, i % 8
    y, x_hi, core = j // 4, (j // 2) % 2, j % 2
    return i, j, x_hi * 2 + x_lo, y, z, core


def at(x, y, z, core):
    return ((x % 2) * 8 + z, y * 4 + (x // 2) * 2 + core)


def flip(value, k):
    total = 0
    for bit in (1, 2, 4):
        b = (value // bit) % 2
        total = total + bit * ((1 - b) if k & bit else b)
    return total


def fill_weights(kern, forward, backward, layer):
    zero = jnp.zeros((3 * LANES, LANES), BF16)
    for ref in (forward, backward):
        ref[0 : 3 * LANES, LANES:] = zero
        ref[9 * LANES :, :LANES] = zero
    for p in range(3):
        for q in range(3):
            k = kern[layer, p, q]
            kt = k.T
            for u in range(2):
                a = ((p + u) * 3 + q) * LANES
                forward[a : a + LANES, u * LANES : (u + 1) * LANES] = k
                b = ((2 - p + u) * 3 + 2 - q) * LANES
                backward[b : b + LANES, u * LANES : (u + 1) * LANES] = kt


def windows(ref, row, s, left=0):
    out = []
    for t in range(4):
        for q in range(3):
            v = ref[pl.ds(row + t * s, s), left + q * s : left + q * s + T]
            out.append(v.reshape(s * T * 16, LANES))
    return jnp.concatenate(out, axis=1)


def stacked(ref, row, s, rows):
    return jnp.concatenate(
        [windows(ref, row + 2 * s * n, s) for n in range(rows // (2 * s))], axis=0
    )


def convolve(ref, weights, row, s, rows):
    both = jnp.dot(stacked(ref, row, s, rows), weights[...], preferred_element_type=F32)
    out = []
    m = T * 16
    for r in range(rows):
        n, u, e = r // (2 * s), (r // s) % 2, r % s
        at0 = (n * s + e) * m
        out.append(both[at0 : at0 + m, u * LANES : (u + 1) * LANES].reshape(T, 16, LANES))
    return out


def swap(low, n0, n1):
    return jnp.where(low, n0, pltpu.roll(n1, 4, 1)), jnp.where(low, pltpu.roll(n0, 4, 1), n1)


def low_half():
    return lax.broadcasted_iota(jnp.int32, (T // 2, 8, LANES), 1) < 4


def into_blocks(ref, c):
    low = low_half()
    n = [ref[CELL * c + e].astype(F32).reshape(T // 2, 8, LANES) for e in range(4)]
    lo = swap(low, n[0], n[1])
    hi = swap(low, n[2], n[3])
    both = [jnp.concatenate([lo[k], hi[k]], axis=1) for k in range(2)]
    return jnp.stack(both, axis=1).reshape(T, 16, LANES)


def out_of_blocks(ref, c, v):
    low = low_half()
    v = v.reshape(T // 2, 2, 16, LANES)
    for h in range(2):
        part = swap(low, v[:, 0, 8 * h : 8 * h + 8], v[:, 1, 8 * h : 8 * h + 8])
        for k in range(2):
            ref[CELL * c + 2 * h + k] = part[k].reshape(T * CELL, LANES).astype(ref.dtype)


def kernel(
    remote, f_hbm, g_hbm, kern, limit_ref, om_hbm, fg_hbm, res,
    fn, gn, f, a1, a1_rows, a1_cols, s1, a2, g2, g2_rows, g2_cols, g1, gf, w1, w1b, w2, w2b, rowm, colm, dw,
    full, got0, wxy, gxy, zbuf,
    local_sem, halo_send, halo_recv, ar_send, ar_recv,
):
    i, j, x, y, z, core = place()
    def inside(dr, dc):
        return (i + dr >= 0) & (i + dr < 16) & (j + dc >= 0) & (j + dc < 16)

    friends = [(lax.rem(i + dr + 16, 16), lax.rem(j + dc + 16, 16)) for dr, dc in SIDES]
    core_friend = at(x, y, z, 1 - core)
    z_friends = [at(x, y, flip(z, k), core) for k in range(1, 8)]
    xy = [(flip(x, k // 4), flip(y, k % 4)) for k in range(1, 16)]
    xy_friends = [at(a, b, z, core) for a, b in xy]
    if remote:
        barrier = pltpu.get_barrier_semaphore()
        everyone = friends + [core_friend] + z_friends + xy_friends
        for d in everyone:
            pl.semaphore_signal(barrier, inc=1, device_id=d, device_id_type=MESH)
    local = [
        pltpu.make_async_copy(f_hbm, fn, local_sem.at[0]),
        pltpu.make_async_copy(g_hbm, gn, local_sem.at[1]),
    ]
    for c in local:
        c.start()
    started = []

    def send(source, target, send_sem, recv_sem, device, go=None):
        c = pltpu.make_async_remote_copy(
            src_ref=source, dst_ref=target, send_sem=send_sem, recv_sem=recv_sem,
            device_id=device, device_id_type=MESH,
        )
        if go is None:
            c.start()
        else:
            pl.when(go)(c.start)
        started.append((c, go))
        return c

    def exchange(n, ref, h):
        if not remote:
            return lambda: None
        src = {-1: pl.ds(h, h), 0: pl.ds(h, T), 1: pl.ds(T, h)}
        dst = {-1: pl.ds(h + T, h), 0: pl.ds(h, T), 1: pl.ds(0, h)}
        copies = [
            send(
                ref.at[src[dr], src[dc]], ref.at[dst[dr], dst[dc]],
                halo_send.at[n, m], halo_recv.at[n, m], friends[m], inside(dr, dc),
            )
            for m, (dr, dc) in enumerate(SIDES)
        ]

        def finish():
            for c, (dr, dc) in zip(copies, SIDES):
                pl.when(inside(-dr, -dc))(c.wait_recv)
            strips = [
                (i == 0, pl.ds(0, h), pl.ds(0, T + 2 * h)),
                (i == 15, pl.ds(T + h, h), pl.ds(0, T + 2 * h)),
                (j == 0, pl.ds(0, T + 2 * h), pl.ds(0, h)),
                (j == 15, pl.ds(0, T + 2 * h), pl.ds(T + h, h)),
            ]
            for edge, r, c in strips:

                @pl.when(edge)
                def _():
                    ref[r, c] = jnp.zeros((r.size, c.size, 16, LANES), BF16)

        return finish

    def strips(n, ref, h, rows, cols):
        for ref_part in (cols.at[:, pl.ds(0, h)], cols.at[:, pl.ds(T + h, h)]):
            ref_part[...] = jnp.zeros((2, h, h, 16, LANES), BF16)
        copies = []
        if remote:
            src = {-1: pl.ds(h, h), 0: pl.ds(h, T), 1: pl.ds(T, h)}
            dst = {-1: pl.ds(h + T, h), 0: pl.ds(h, T), 1: pl.ds(0, h)}
            for m, (dr, dc) in enumerate(SIDES):
                if dr:
                    target = rows.at[(1 - dr) // 2, pl.ds(0, h), dst[dc]]
                else:
                    target = cols.at[(1 - dc) // 2, dst[0]]
                copies.append(
                    send(
                        ref.at[src[dr], src[dc]], target,
                        halo_send.at[n, m], halo_recv.at[n, m], friends[m], inside(dr, dc),
                    )
                )

        def finish():
            for c, (dr, dc) in zip(copies, SIDES):
                pl.when(inside(-dr, -dc))(c.wait_recv)
            for k, edge in enumerate((0, 15)):

                @pl.when(i == edge)
                def _():
                    rows[k] = jnp.zeros((h, T + 2 * h, 16, LANES), BF16)

                @pl.when(j == edge)
                def _():
                    rows[:, :, k * (T + h) : k * (T + h) + h] = jnp.zeros(
                        (2, h, h, 16, LANES), BF16
                    )
                    cols[k] = jnp.zeros((T + 2 * h, h, 16, LANES), BF16)

            for k in range(2):
                lo = k * (T + h)
                ref[h : T + h, lo : lo + h] = cols[k, h : T + h]
                ref[lo : lo + h] = rows[k]

        return finish

    def borders(weights, h, rows, cols):
        def product(parts, taps):
            lhs = jnp.concatenate([v.reshape(h * T * 16, LANES) for v in parts], axis=1)
            rhs = jnp.concatenate(
                [weights[n * LANES : (n + 1) * LANES, :LANES] for n in taps], axis=0
            )
            return jnp.dot(lhs, rhs, preferred_element_type=F32)

        out = []
        for k in range(2):
            v = product(
                [rows[k, :, q * h : q * h + T] for q in range(3)],
                [2 * k * 3 + q for q in range(3)],
            )
            out.append((pl.ds(k * (T - h), h), pl.ds(0, T), v.reshape(h, T, 16, LANES)))
        for k in range(2):
            v = product(
                [cols[k, p * h : p * h + T] for p in range(3)],
                [p * 3 + 2 * k for p in range(3)],
            )
            out.append((pl.ds(0, T), pl.ds(k * (T - h), h), v.reshape(T, h, 16, LANES)))
        return out

    def zero_border(ref, h):
        ref[0:h] = jnp.zeros((h, T + 2 * h, 16, LANES), BF16)
        ref[T + h :] = jnp.zeros((h, T + 2 * h, 16, LANES), BF16)
        ref[:, 0:h] = jnp.zeros((T + 2 * h, h, 16, LANES), BF16)
        ref[:, T + h :] = jnp.zeros((T + 2 * h, h, 16, LANES), BF16)

    def live(r, c):
        return rowm[r][:, None] * colm[c][None]

    def shifted(d, n):
        return pl.ds(d.start + n, d.size)

    limit = limit_ref[0]
    sub = lax.broadcasted_iota(jnp.int32, (T, 16, LANES), 1)
    blk = lax.broadcasted_iota(jnp.int32, (T, 16, LANES), 0) * CELL
    rowm[...] = jnp.where(blk + sub // CELL + i * (T * CELL) < limit, 1.0, 0.0).astype(F32)
    colm[...] = jnp.where(blk + sub % CELL + j * (T * CELL) < limit, 1.0, 0.0).astype(F32)
    own1, own2 = pl.ds(ONE, T), pl.ds(TWO, T)

    def prepare_f(c, _):
        v = into_blocks(fn, c)
        f[c] = v.astype(BF16)
        a1[c + ONE, own1] = (elu(v) * (rowm[c] * colm[...])).astype(BF16)
        return 0

    def prepare_g(c, _):
        v = into_blocks(gn, c)
        g2[c + TWO, own2] = (v * (rowm[c] * colm[...])).astype(BF16)
        return 0

    zero_border(a1, ONE)
    zero_border(g2, TWO)
    local[0].wait()
    lax.fori_loop(0, T, prepare_f, 0)
    if remote:
        pl.semaphore_wait(barrier, len(everyone))
    finish_a1 = strips(0, a1, ONE, a1_rows, a1_cols)
    local[1].wait()
    lax.fori_loop(0, T, prepare_g, 0)
    finish_g2 = strips(1, g2, TWO, g2_rows, g2_cols)
    fill_weights(kern, w1, w1b, 0)
    fill_weights(kern, w2, w2b, 1)

    def conv1(k, _):
        for e, v in enumerate(convolve(a1, w1, k * R, ONE, R)):
            r = k * R + e
            v = v + f[r].astype(F32)
            s1[r] = v
            a2[r + TWO, own2] = (elu(v) * (rowm[r] * colm[...])).astype(BF16)
        return 0

    lax.fori_loop(0, T // R, conv1, 0)
    finish_a1()
    edges = borders(w1, ONE, a1_rows, a1_cols)
    for r, c, v in edges:
        s1[r, c] += v
    for r, c, _ in edges:
        a2[shifted(r, TWO), shifted(c, TWO)] = (elu(s1[r, c]) * live(r, c)).astype(BF16)

    def contract(own, o, wide, s, layer, turned):
        lhs = []
        for n in range(T // (2 * s)):
            b = 2 * s * n
            gs = [
                own[pl.ds(b + o + u * s, s), o : o + T].reshape(s * T * 16, LANES)
                for u in range(2)
            ]
            lhs.append(jnp.concatenate(gs, axis=1))
        lhs = jnp.concatenate(lhs, axis=0)
        rhs = stacked(wide, 0, s, T)
        dw[...] = lax.dot_general(lhs, rhs, (((0,), (0,)), ((), ())), preferred_element_type=F32)
        for p in range(3):
            for q in range(3):
                a, b = (p, q) if turned else (2 - p, 2 - q)
                lo = (a * 3 + b) * LANES
                hi = ((a + 1) * 3 + b) * LANES
                v = dw[:LANES, lo : lo + LANES] + dw[LANES:, hi : hi + LANES]
                v = (v.T if turned else v).reshape(2, 8, 8, LANES)
                for h in range(2):
                    n = (p * 3 + q) * 16 + 8 * h
                    full[layer, n // HALF, n % HALF : n % HALF + 8] = v[h]
        full[layer, :, HALF:] = jnp.zeros((2, PADDED - HALF, 8, LANES), F32)

    mine = x * 4 + y
    mine_at = pl.ds(mine * PIECE, PIECE)

    class Reduction:
        def __init__(self, layer):
            self.layer, self.slot, self.pending = layer, 0, []

        def send(self, source, target, device):
            n = self.slot
            self.slot += 1
            sems = ar_send.at[self.layer, n], ar_recv.at[self.layer, n]
            self.pending.append(send(source, target, *sems, device))

        def arrive(self):
            for c in self.pending:
                c.wait_recv()
            self.pending = []

        def core_out(self):
            n = self.layer
            if remote:
                self.send(full.at[n, 1 - core], got0.at[n], core_friend)

        def plane_out(self):
            n = self.layer
            if not remote:
                return
            self.arrive()
            v = full[n, core] + got0[n]
            full[n, core] = v
            wxy[n] = v.reshape(16, PIECE, 8, LANES).astype(WIRE)
            for k in FAR_FIRST:
                a, b = xy[k]
                self.send(wxy.at[n, a * 4 + b], gxy.at[n, k], xy_friends[k])

        def z_out(self):
            n = self.layer
            if not remote:
                return
            self.arrive()
            v = full[n, core, mine_at]
            for k in range(15):
                v = v + gxy[n, k].astype(F32)
            zbuf[n, z] = v.astype(WIRE)
            for k in (4, 5, 3, 7, 6, 2, 1):
                self.send(zbuf.at[n, z], zbuf.at[n, z], z_friends[k - 1])

        def plane_back(self):
            n = self.layer
            if not remote:
                return
            self.arrive()
            v = zbuf[n, 0].astype(F32)
            for k in range(1, 8):
                v = v + zbuf[n, k].astype(F32)
            res[n, core, mine_at] = (v / limit.astype(F32)).astype(WIRE)
            piece = res.at[n, core, mine_at]
            for k in FAR_FIRST:
                self.send(piece, piece, xy_friends[k])
            self.coming, self.pending = dict(zip(FAR_FIRST, self.pending)), []
            self.send(piece, piece, core_friend)

        def core_back(self):
            n = self.layer
            if not remote:
                res[n] = (full[n] / limit.astype(F32)).astype(WIRE)
                return
            for k in sorted(range(15), key=lambda k: HOPS[k]):
                self.coming[k].wait_recv()
                a, b = xy[k]
                piece = res.at[n, core, pl.ds((a * 4 + b) * PIECE, PIECE)]
                self.send(piece, piece, core_friend)

    second, first = Reduction(1), Reduction(0)

    def back2(k, _):
        for e, v in enumerate(convolve(g2, w2b, k * R, TWO, R)):
            r = k * R + e
            m = rowm[r] * colm[...]
            v = g2[r + TWO, own2].astype(F32) + m * slope(s1[r]) * v
            gf[r] = v
            g1[r + ONE, own1] = v.astype(BF16)
        return 0

    lax.fori_loop(0, T // R, back2, 0)
    finish_g2()
    edges = borders(w2b, TWO, g2_rows, g2_cols)
    for r, c, v in edges:
        gf[r, c] += live(r, c) * slope(s1[r, c]) * v
    for r, c, _ in edges:
        g1[shifted(r, ONE), shifted(c, ONE)] = gf[r, c].astype(BF16)
    finish_g1 = exchange(3, g1, ONE)
    contract(a2, TWO, g2, TWO, 1, False)
    second.core_out()
    contract(g1, ONE, a1, ONE, 0, True)
    first.core_out()
    second.plane_out()

    def conv2(k, _):
        for e, v in enumerate(convolve(a2, w2, k * R, TWO, R)):
            r = k * R + e
            out_of_blocks(fn, r, rowm[r] * colm[...] * (s1[r] + v))
        return 0

    def back1(k, _):
        for e, v in enumerate(convolve(g1, w1b, k * R, ONE, R)):
            r = k * R + e
            m = rowm[r] * colm[...]
            out_of_blocks(gn, r, gf[r] + m * slope(f[r].astype(F32)) * v)
        return 0

    first.plane_out()
    finish_a2 = exchange(2, a2, TWO)
    second.z_out()
    first.z_out()
    finish_g1()
    lax.fori_loop(0, T // R, back1, 0)
    fg = pltpu.make_async_copy(gn, fg_hbm, local_sem.at[3])
    fg.start()
    second.plane_back()
    first.plane_back()
    finish_a2()
    lax.fori_loop(0, T // R, conv2, 0)
    om = pltpu.make_async_copy(fn, om_hbm, local_sem.at[2])
    om.start()
    second.core_back()
    first.core_back()
    om.wait()
    fg.wait()
    second.arrive()
    first.arrive()
    for c, go in started:
        if go is None:
            c.wait_send()
        else:
            pl.when(go)(c.wait_send)


R = 8


def call(remote, f, g, kernels, length):
    vm = pltpu.VMEM
    sems = pltpu.SemaphoreType.DMA
    tile = (T * CELL, T * CELL, LANES)

    def blocks(h, kind):
        return vm((T + 2 * h, T + 2 * h, 16, LANES), kind)

    return pl.pallas_call(
        functools.partial(kernel, remote),
        out_shape=(
            jax.ShapeDtypeStruct(tile, BF16),
            jax.ShapeDtypeStruct(tile, BF16),
            jax.ShapeDtypeStruct((2, 2, PADDED, 8, LANES), WIRE),
        ),
        in_specs=[
            pl.BlockSpec(memory_space=pltpu.HBM),
            pl.BlockSpec(memory_space=pltpu.HBM),
            pl.BlockSpec(memory_space=pltpu.VMEM),
            pl.BlockSpec(memory_space=pltpu.SMEM),
        ],
        out_specs=[
            pl.BlockSpec(memory_space=pl.ANY),
            pl.BlockSpec(memory_space=pl.ANY),
            pl.BlockSpec(memory_space=pltpu.VMEM),
        ],
        scratch_shapes=[
            vm(tile, BF16),
            vm(tile, BF16),
            blocks(0, BF16),
            blocks(ONE, BF16),
            vm((2, ONE, T + 2 * ONE, 16, LANES), BF16),
            vm((2, T + 2 * ONE, ONE, 16, LANES), BF16),
            blocks(0, F32),
            blocks(TWO, BF16),
            blocks(TWO, BF16),
            vm((2, TWO, T + 2 * TWO, 16, LANES), BF16),
            vm((2, T + 2 * TWO, TWO, 16, LANES), BF16),
            blocks(ONE, BF16),
            blocks(0, F32),
            vm((12 * LANES, 2 * LANES), BF16),
            vm((12 * LANES, 2 * LANES), BF16),
            vm((12 * LANES, 2 * LANES), BF16),
            vm((12 * LANES, 2 * LANES), BF16),
            vm((T, 16, LANES), F32),
            vm((T, 16, LANES), F32),
            vm((2 * LANES, 12 * LANES), F32),
            vm((2, 2, PADDED, 8, LANES), F32),
            vm((2, PADDED, 8, LANES), F32),
            vm((2, 16, PIECE, 8, LANES), WIRE),
            vm((2, 15, PIECE, 8, LANES), WIRE),
            vm((2, 8, PIECE, 8, LANES), WIRE),
            sems((4,)),
            sems((4, 8)),
            sems((4, 8)),
            sems((2, 54)),
            sems((2, 54)),
        ],
        compiler_params=pltpu.CompilerParams(
            collective_id=0 if remote else None, has_side_effects=True, vmem_limit_bytes=50 << 20
        ),
    )(f, g, kernels, length)


def place_kernel(om_in, fg_in, kg_in, om_out, fg_out, kg_out, k, wide, sems):
    moves = [(kg_in, k), (om_in, om_out), (fg_in, fg_out)]
    copies = [
        pltpu.make_async_copy(source, target, sems.at[n])
        for n, (source, target) in enumerate(moves)
    ]
    for c in copies:
        c.start()
    copies[0].wait()
    wide[...] = k[:, :, :HALF].astype(F32)
    last = pltpu.make_async_copy(wide, kg_out, sems.at[3])
    last.start()
    for c in copies[1:]:
        c.wait()
    last.wait()


def body(features, kernels, length, cotangent):
    om, fg, kg = call(True, features, cotangent, kernels, length)
    vm = pltpu.VMEM
    om, fg, kg = pl.pallas_call(
        place_kernel,
        out_shape=(
            jax.ShapeDtypeStruct(om.shape, om.dtype),
            jax.ShapeDtypeStruct(fg.shape, fg.dtype),
            jax.ShapeDtypeStruct((2, 2, HALF, 8, LANES), F32),
        ),
        in_specs=[pl.BlockSpec(memory_space=pl.ANY)] * 3,
        out_specs=[pl.BlockSpec(memory_space=pl.ANY)] * 3,
        scratch_shapes=[
            vm(kg.shape, kg.dtype),
            vm((2, 2, HALF, 8, LANES), F32),
            pltpu.SemaphoreType.DMA((4,)),
        ],
        compiler_params=pltpu.CompilerParams(vmem_limit_bytes=8 << 20),
    )(om, fg, kg)
    return om, fg, kg.reshape(kernels.shape)


def solution(mesh):
    in_specs = (P("row", "col", None), P(), P(), P("row", "col", None))
    out_specs = (P("row", "col", None), P("row", "col", None), P())
    return jax.shard_map(body, mesh=mesh, in_specs=in_specs, out_specs=out_specs, check_vma=False)
```

```python
import functools

import jax
import jax.numpy as jnp
from jax import lax
from jax.experimental import pallas as pl
from jax.experimental.pallas import tpu as pltpu
from jax.sharding import PartitionSpec as P

MESH = pl.DeviceIdType.MESH
F32, BF16 = jnp.float32, jnp.bfloat16
FIRST_SPACING = 4
SECOND_SPACING = 8
CELL = 4
ONE, TWO = FIRST_SPACING // CELL, SECOND_SPACING // CELL
T = 16
LANES = 128
CORNERS = [(-1, -1), (-1, 1), (1, -1), (1, 1)]
SIDES = CORNERS + [(0, -1), (0, 1), (-1, 0), (1, 0)]
HALF = 72
PIECE = 5
PADDED = 16 * PIECE
WIRE = BF16
HOPS = [(0, 1, 2, 1)[k // 4] + (0, 1, 2, 1)[k % 4] for k in range(1, 16)]
FAR_FIRST = sorted(range(15), key=lambda k: -HOPS[k])


def exp_low(values):
    return jnp.exp(jnp.minimum(values, 0.0))


def elu(values):
    return jnp.where(values > 0, values, exp_low(values) - 1.0)


def slope(values):
    return jnp.where(values > 0, 1.0, exp_low(values))


def place():
    i, j = lax.axis_index("row"), lax.axis_index("col")
    x_lo, z = i // 8, i % 8
    y, x_hi, core = j // 4, (j // 2) % 2, j % 2
    return i, j, x_hi * 2 + x_lo, y, z, core


def at(x, y, z, core):
    return ((x % 2) * 8 + z, y * 4 + (x // 2) * 2 + core)


def flip(value, k):
    total = 0
    for bit in (1, 2, 4):
        b = (value // bit) % 2
        total = total + bit * ((1 - b) if k & bit else b)
    return total


def fill_weights(kern, forward, backward, layer):
    zero = jnp.zeros((3 * LANES, LANES), BF16)
    for ref in (forward, backward):
        ref[0 : 3 * LANES, LANES:] = zero
        ref[9 * LANES :, :LANES] = zero
    for p in range(3):
        for q in range(3):
            k = kern[layer, p, q]
            kt = k.T
            for u in range(2):
                a = ((p + u) * 3 + q) * LANES
                forward[a : a + LANES, u * LANES : (u + 1) * LANES] = k
                b = ((2 - p + u) * 3 + 2 - q) * LANES
                backward[b : b + LANES, u * LANES : (u + 1) * LANES] = kt


def windows(ref, row, s, left=0):
    out = []
    for t in range(4):
        for q in range(3):
            v = ref[pl.ds(row + t * s, s), left + q * s : left + q * s + T]
            out.append(v.reshape(s * T * 16, LANES))
    return jnp.concatenate(out, axis=1)


def stacked(ref, row, s, rows):
    return jnp.concatenate(
        [windows(ref, row + 2 * s * n, s) for n in range(rows // (2 * s))], axis=0
    )


def convolve(ref, weights, row, s, rows):
    both = jnp.dot(stacked(ref, row, s, rows), weights[...], preferred_element_type=F32)
    out = []
    m = T * 16
    for r in range(rows):
        n, u, e = r // (2 * s), (r // s) % 2, r % s
        at0 = (n * s + e) * m
        out.append(both[at0 : at0 + m, u * LANES : (u + 1) * LANES].reshape(T, 16, LANES))
    return out


def swap(low, n0, n1):
    return jnp.where(low, n0, pltpu.roll(n1, 4, 1)), jnp.where(low, pltpu.roll(n0, 4, 1), n1)


def low_half():
    return lax.broadcasted_iota(jnp.int32, (T // 2, 8, LANES), 1) < 4


def into_blocks(ref, c):
    low = low_half()
    n = [ref[CELL * c + e].astype(F32).reshape(T // 2, 8, LANES) for e in range(4)]
    lo = swap(low, n[0], n[1])
    hi = swap(low, n[2], n[3])
    both = [jnp.concatenate([lo[k], hi[k]], axis=1) for k in range(2)]
    return jnp.stack(both, axis=1).reshape(T, 16, LANES)


def out_of_blocks(ref, c, v):
    low = low_half()
    v = v.reshape(T // 2, 2, 16, LANES)
    for h in range(2):
        part = swap(low, v[:, 0, 8 * h : 8 * h + 8], v[:, 1, 8 * h : 8 * h + 8])
        for k in range(2):
            ref[CELL * c + 2 * h + k] = part[k].reshape(T * CELL, LANES).astype(ref.dtype)


def kernel(
    remote, f_hbm, g_hbm, kern, limit_ref, om_hbm, fg_hbm, res,
    fn, gn, f, a1, a1_rows, a1_cols, s1, a2, g2, g2_rows, g2_cols, g1, gf, w1, w1b, w2, w2b, rowm, colm, dw,
    full, got0, wxy, gxy, zbuf,
    local_sem, halo_send, halo_recv, ar_send, ar_recv,
):
    i, j, x, y, z, core = place()
    def inside(dr, dc):
        return (i + dr >= 0) & (i + dr < 16) & (j + dc >= 0) & (j + dc < 16)

    friends = [(lax.rem(i + dr + 16, 16), lax.rem(j + dc + 16, 16)) for dr, dc in SIDES]
    core_friend = at(x, y, z, 1 - core)
    z_friends = [at(x, y, flip(z, k), core) for k in range(1, 8)]
    xy = [(flip(x, k // 4), flip(y, k % 4)) for k in range(1, 16)]
    xy_friends = [at(a, b, z, core) for a, b in xy]
    if remote:
        barrier = pltpu.get_barrier_semaphore()
        everyone = friends + [core_friend] + z_friends + xy_friends
        for d in everyone:
            pl.semaphore_signal(barrier, inc=1, device_id=d, device_id_type=MESH)
    local = [
        pltpu.make_async_copy(f_hbm, fn, local_sem.at[0]),
        pltpu.make_async_copy(g_hbm, gn, local_sem.at[1]),
    ]
    for c in local:
        c.start()
    started = []

    def send(source, target, send_sem, recv_sem, device, go=None):
        c = pltpu.make_async_remote_copy(
            src_ref=source, dst_ref=target, send_sem=send_sem, recv_sem=recv_sem,
            device_id=device, device_id_type=MESH,
        )
        if go is None:
            c.start()
        else:
            pl.when(go)(c.start)
        started.append((c, go))
        return c

    def exchange(n, ref, h):
        if not remote:
            return lambda: None
        src = {-1: pl.ds(h, h), 0: pl.ds(h, T), 1: pl.ds(T, h)}
        dst = {-1: pl.ds(h + T, h), 0: pl.ds(h, T), 1: pl.ds(0, h)}
        copies = [
            send(
                ref.at[src[dr], src[dc]], ref.at[dst[dr], dst[dc]],
                halo_send.at[n, m], halo_recv.at[n, m], friends[m], inside(dr, dc),
            )
            for m, (dr, dc) in enumerate(SIDES)
        ]

        def finish():
            for c, (dr, dc) in zip(copies, SIDES):
                pl.when(inside(-dr, -dc))(c.wait_recv)
            strips = [
                (i == 0, pl.ds(0, h), pl.ds(0, T + 2 * h)),
                (i == 15, pl.ds(T + h, h), pl.ds(0, T + 2 * h)),
                (j == 0, pl.ds(0, T + 2 * h), pl.ds(0, h)),
                (j == 15, pl.ds(0, T + 2 * h), pl.ds(T + h, h)),
            ]
            for edge, r, c in strips:

                @pl.when(edge)
                def _():
                    ref[r, c] = jnp.zeros((r.size, c.size, 16, LANES), BF16)

        return finish

    def strips(n, ref, h, rows, cols):
        for ref_part in (cols.at[:, pl.ds(0, h)], cols.at[:, pl.ds(T + h, h)]):
            ref_part[...] = jnp.zeros((2, h, h, 16, LANES), BF16)
        copies = []
        if remote:
            src = {-1: pl.ds(h, h), 0: pl.ds(h, T), 1: pl.ds(T, h)}
            dst = {-1: pl.ds(h + T, h), 0: pl.ds(h, T), 1: pl.ds(0, h)}
            for m, (dr, dc) in enumerate(SIDES):
                if dr:
                    target = rows.at[(1 - dr) // 2, pl.ds(0, h), dst[dc]]
                else:
                    target = cols.at[(1 - dc) // 2, dst[0]]
                copies.append(
                    send(
                        ref.at[src[dr], src[dc]], target,
                        halo_send.at[n, m], halo_recv.at[n, m], friends[m], inside(dr, dc),
                    )
                )

        def finish():
            for c, (dr, dc) in zip(copies, SIDES):
                pl.when(inside(-dr, -dc))(c.wait_recv)
            for k, edge in enumerate((0, 15)):

                @pl.when(i == edge)
                def _():
                    rows[k] = jnp.zeros((h, T + 2 * h, 16, LANES), BF16)

                @pl.when(j == edge)
                def _():
                    rows[:, :, k * (T + h) : k * (T + h) + h] = jnp.zeros(
                        (2, h, h, 16, LANES), BF16
                    )
                    cols[k] = jnp.zeros((T + 2 * h, h, 16, LANES), BF16)

            for k in range(2):
                lo = k * (T + h)
                ref[h : T + h, lo : lo + h] = cols[k, h : T + h]
                ref[lo : lo + h] = rows[k]

        return finish

    def borders(weights, h, rows, cols):
        def product(parts, taps):
            lhs = jnp.concatenate([v.reshape(h * T * 16, LANES) for v in parts], axis=1)
            rhs = jnp.concatenate(
                [weights[n * LANES : (n + 1) * LANES, :LANES] for n in taps], axis=0
            )
            return jnp.dot(lhs, rhs, preferred_element_type=F32)

        out = []
        for k in range(2):
            v = product(
                [rows[k, :, q * h : q * h + T] for q in range(3)],
                [2 * k * 3 + q for q in range(3)],
            )
            out.append((pl.ds(k * (T - h), h), pl.ds(0, T), v.reshape(h, T, 16, LANES)))
        for k in range(2):
            v = product(
                [cols[k, p * h : p * h + T] for p in range(3)],
                [p * 3 + 2 * k for p in range(3)],
            )
            out.append((pl.ds(0, T), pl.ds(k * (T - h), h), v.reshape(T, h, 16, LANES)))
        return out

    def zero_border(ref, h):
        ref[0:h] = jnp.zeros((h, T + 2 * h, 16, LANES), BF16)
        ref[T + h :] = jnp.zeros((h, T + 2 * h, 16, LANES), BF16)
        ref[:, 0:h] = jnp.zeros((T + 2 * h, h, 16, LANES), BF16)
        ref[:, T + h :] = jnp.zeros((T + 2 * h, h, 16, LANES), BF16)

    def live(r, c):
        return rowm[r][:, None] * colm[c][None]

    def shifted(d, n):
        return pl.ds(d.start + n, d.size)

    limit = limit_ref[0]
    sub = lax.broadcasted_iota(jnp.int32, (T, 16, LANES), 1)
    blk = lax.broadcasted_iota(jnp.int32, (T, 16, LANES), 0) * CELL
    rowm[...] = jnp.where(blk + sub // CELL + i * (T * CELL) < limit, 1.0, 0.0).astype(F32)
    colm[...] = jnp.where(blk + sub % CELL + j * (T * CELL) < limit, 1.0, 0.0).astype(F32)
    own1, own2 = pl.ds(ONE, T), pl.ds(TWO, T)

    def prepare_f(c, _):
        v = into_blocks(fn, c)
        f[c] = v.astype(BF16)
        a1[c + ONE, own1] = (elu(v) * (rowm[c] * colm[...])).astype(BF16)
        return 0

    def prepare_g(c, _):
        v = into_blocks(gn, c)
        g2[c + TWO, own2] = (v * (rowm[c] * colm[...])).astype(BF16)
        return 0

    zero_border(a1, ONE)
    zero_border(g2, TWO)
    local[0].wait()
    lax.fori_loop(0, T, prepare_f, 0)
    if remote:
        pl.semaphore_wait(barrier, len(everyone))
    finish_a1 = strips(0, a1, ONE, a1_rows, a1_cols)
    local[1].wait()
    lax.fori_loop(0, T, prepare_g, 0)
    finish_g2 = strips(1, g2, TWO, g2_rows, g2_cols)
    fill_weights(kern, w1, w1b, 0)
    fill_weights(kern, w2, w2b, 1)

    def conv1(k, _):
        for e, v in enumerate(convolve(a1, w1, k * R, ONE, R)):
            r = k * R + e
            v = v + f[r].astype(F32)
            s1[r] = v
            a2[r + TWO, own2] = (elu(v) * (rowm[r] * colm[...])).astype(BF16)
        return 0

    lax.fori_loop(0, T // R, conv1, 0)
    finish_a1()
    edges = borders(w1, ONE, a1_rows, a1_cols)
    for r, c, v in edges:
        s1[r, c] += v
    for r, c, _ in edges:
        a2[shifted(r, TWO), shifted(c, TWO)] = (elu(s1[r, c]) * live(r, c)).astype(BF16)

    def contract(own, o, wide, s, layer, turned):
        lhs = []
        for n in range(T // (2 * s)):
            b = 2 * s * n
            gs = [
                own[pl.ds(b + o + u * s, s), o : o + T].reshape(s * T * 16, LANES)
                for u in range(2)
            ]
            lhs.append(jnp.concatenate(gs, axis=1))
        lhs = jnp.concatenate(lhs, axis=0)
        rhs = stacked(wide, 0, s, T)
        dw[...] = lax.dot_general(lhs, rhs, (((0,), (0,)), ((), ())), preferred_element_type=F32)
        for p in range(3):
            for q in range(3):
                a, b = (p, q) if turned else (2 - p, 2 - q)
                lo = (a * 3 + b) * LANES
                hi = ((a + 1) * 3 + b) * LANES
                v = dw[:LANES, lo : lo + LANES] + dw[LANES:, hi : hi + LANES]
                v = (v.T if turned else v).reshape(2, 8, 8, LANES)
                for h in range(2):
                    n = (p * 3 + q) * 16 + 8 * h
                    full[layer, n // HALF, n % HALF : n % HALF + 8] = v[h]
        full[layer, :, HALF:] = jnp.zeros((2, PADDED - HALF, 8, LANES), F32)

    mine = x * 4 + y
    mine_at = pl.ds(mine * PIECE, PIECE)

    class Reduction:
        def __init__(self, layer):
            self.layer, self.slot, self.pending = layer, 0, []

        def send(self, source, target, device):
            n = self.slot
            self.slot += 1
            sems = ar_send.at[self.layer, n], ar_recv.at[self.layer, n]
            self.pending.append(send(source, target, *sems, device))

        def arrive(self):
            for c in self.pending:
                c.wait_recv()
            self.pending = []

        def core_out(self):
            n = self.layer
            if remote:
                self.send(full.at[n, 1 - core], got0.at[n], core_friend)

        def plane_out(self):
            n = self.layer
            if not remote:
                return
            self.arrive()
            v = full[n, core] + got0[n]
            full[n, core] = v
            wxy[n] = v.reshape(16, PIECE, 8, LANES).astype(WIRE)
            for k in FAR_FIRST:
                a, b = xy[k]
                self.send(wxy.at[n, a * 4 + b], gxy.at[n, k], xy_friends[k])

        def z_out(self):
            n = self.layer
            if not remote:
                return
            self.arrive()
            v = full[n, core, mine_at]
            for k in range(15):
                v = v + gxy[n, k].astype(F32)
            zbuf[n, z] = v.astype(WIRE)
            for k in (4, 5, 3, 7, 6, 2, 1):
                self.send(zbuf.at[n, z], zbuf.at[n, z], z_friends[k - 1])

        def plane_back(self):
            n = self.layer
            if not remote:
                return
            self.arrive()
            v = zbuf[n, 0].astype(F32)
            for k in range(1, 8):
                v = v + zbuf[n, k].astype(F32)
            res[n, core, mine_at] = (v / limit.astype(F32)).astype(WIRE)
            piece = res.at[n, core, mine_at]
            for k in FAR_FIRST:
                self.send(piece, piece, xy_friends[k])
            self.coming, self.pending = dict(zip(FAR_FIRST, self.pending)), []
            self.send(piece, piece, core_friend)

        def core_back(self):
            n = self.layer
            if not remote:
                res[n] = (full[n] / limit.astype(F32)).astype(WIRE)
                return
            for k in sorted(range(15), key=lambda k: HOPS[k]):
                self.coming[k].wait_recv()
                a, b = xy[k]
                piece = res.at[n, core, pl.ds((a * 4 + b) * PIECE, PIECE)]
                self.send(piece, piece, core_friend)

    second, first = Reduction(1), Reduction(0)

    def back2(k, _):
        for e, v in enumerate(convolve(g2, w2b, k * R, TWO, R)):
            r = k * R + e
            m = rowm[r] * colm[...]
            v = g2[r + TWO, own2].astype(F32) + m * slope(s1[r]) * v
            gf[r] = v
            g1[r + ONE, own1] = v.astype(BF16)
        return 0

    lax.fori_loop(0, T // R, back2, 0)
    finish_g2()
    edges = borders(w2b, TWO, g2_rows, g2_cols)
    for r, c, v in edges:
        gf[r, c] += live(r, c) * slope(s1[r, c]) * v
    for r, c, _ in edges:
        g1[shifted(r, ONE), shifted(c, ONE)] = gf[r, c].astype(BF16)
    finish_g1 = exchange(3, g1, ONE)
    contract(a2, TWO, g2, TWO, 1, False)
    second.core_out()
    contract(g1, ONE, a1, ONE, 0, True)
    first.core_out()
    second.plane_out()

    def conv2(k, _):
        for e, v in enumerate(convolve(a2, w2, k * R, TWO, R)):
            r = k * R + e
            out_of_blocks(fn, r, rowm[r] * colm[...] * (s1[r] + v))
        return 0

    def back1(k, _):
        for e, v in enumerate(convolve(g1, w1b, k * R, ONE, R)):
            r = k * R + e
            m = rowm[r] * colm[...]
            out_of_blocks(gn, r, gf[r] + m * slope(f[r].astype(F32)) * v)
        return 0

    first.plane_out()
    finish_a2 = exchange(2, a2, TWO)
    second.z_out()
    first.z_out()
    finish_g1()
    lax.fori_loop(0, T // R, back1, 0)
    fg = pltpu.make_async_copy(gn, fg_hbm, local_sem.at[3])
    fg.start()
    second.plane_back()
    first.plane_back()
    finish_a2()
    lax.fori_loop(0, T // R, conv2, 0)
    om = pltpu.make_async_copy(fn, om_hbm, local_sem.at[2])
    om.start()
    second.core_back()
    first.core_back()
    om.wait()
    fg.wait()
    second.arrive()
    first.arrive()
    for c, go in started:
        if go is None:
            c.wait_send()
        else:
            pl.when(go)(c.wait_send)


R = 8


def call(remote, f, g, kernels, length):
    vm = pltpu.VMEM
    sems = pltpu.SemaphoreType.DMA
    tile = (T * CELL, T * CELL, LANES)

    def blocks(h, kind):
        return vm((T + 2 * h, T + 2 * h, 16, LANES), kind)

    return pl.pallas_call(
        functools.partial(kernel, remote),
        out_shape=(
            jax.ShapeDtypeStruct(tile, BF16),
            jax.ShapeDtypeStruct(tile, BF16),
            jax.ShapeDtypeStruct((2, 2, PADDED, 8, LANES), WIRE),
        ),
        in_specs=[
            pl.BlockSpec(memory_space=pltpu.HBM),
            pl.BlockSpec(memory_space=pltpu.HBM),
            pl.BlockSpec(memory_space=pltpu.VMEM),
            pl.BlockSpec(memory_space=pltpu.SMEM),
        ],
        out_specs=[
            pl.BlockSpec(memory_space=pl.ANY),
            pl.BlockSpec(memory_space=pl.ANY),
            pl.BlockSpec(memory_space=pltpu.VMEM),
        ],
        scratch_shapes=[
            vm(tile, BF16),
            vm(tile, BF16),
            blocks(0, BF16),
            blocks(ONE, BF16),
            vm((2, ONE, T + 2 * ONE, 16, LANES), BF16),
            vm((2, T + 2 * ONE, ONE, 16, LANES), BF16),
            blocks(0, F32),
            blocks(TWO, BF16),
            blocks(TWO, BF16),
            vm((2, TWO, T + 2 * TWO, 16, LANES), BF16),
            vm((2, T + 2 * TWO, TWO, 16, LANES), BF16),
            blocks(ONE, BF16),
            blocks(0, F32),
            vm((12 * LANES, 2 * LANES), BF16),
            vm((12 * LANES, 2 * LANES), BF16),
            vm((12 * LANES, 2 * LANES), BF16),
            vm((12 * LANES, 2 * LANES), BF16),
            vm((T, 16, LANES), F32),
            vm((T, 16, LANES), F32),
            vm((2 * LANES, 12 * LANES), F32),
            vm((2, 2, PADDED, 8, LANES), F32),
            vm((2, PADDED, 8, LANES), F32),
            vm((2, 16, PIECE, 8, LANES), WIRE),
            vm((2, 15, PIECE, 8, LANES), WIRE),
            vm((2, 8, PIECE, 8, LANES), WIRE),
            sems((4,)),
            sems((4, 8)),
            sems((4, 8)),
            sems((2, 54)),
            sems((2, 54)),
        ],
        compiler_params=pltpu.CompilerParams(
            collective_id=0 if remote else None, has_side_effects=True, vmem_limit_bytes=50 << 20
        ),
    )(f, g, kernels, length)


def place_kernel(om_in, fg_in, kg_in, om_out, fg_out, kg_out, k, wide, sems):
    moves = [(kg_in, k), (om_in, om_out), (fg_in, fg_out)]
    copies = [
        pltpu.make_async_copy(source, target, sems.at[n])
        for n, (source, target) in enumerate(moves)
    ]
    for c in copies:
        c.start()
    copies[0].wait()
    wide[...] = k[:, :, :HALF].astype(F32)
    last = pltpu.make_async_copy(wide, kg_out, sems.at[3])
    last.start()
    for c in copies[1:]:
        c.wait()
    last.wait()


def body(features, kernels, length, cotangent):
    om, fg, kg = call(True, features, cotangent, kernels, length)
    vm = pltpu.VMEM
    om, fg, kg = pl.pallas_call(
        place_kernel,
        out_shape=(
            jax.ShapeDtypeStruct(om.shape, om.dtype),
            jax.ShapeDtypeStruct(fg.shape, fg.dtype),
            jax.ShapeDtypeStruct((2, 2, HALF, 8, LANES), F32),
        ),
        in_specs=[pl.BlockSpec(memory_space=pl.ANY)] * 3,
        out_specs=[pl.BlockSpec(memory_space=pl.ANY)] * 3,
        scratch_shapes=[
            vm(kg.shape, kg.dtype),
            vm((2, 2, HALF, 8, LANES), F32),
            pltpu.SemaphoreType.DMA((4,)),
        ],
        compiler_params=pltpu.CompilerParams(vmem_limit_bytes=8 << 20),
    )(om, fg, kg)
    return om, fg, kg.reshape(kernels.shape)


def solution(mesh):
    in_specs = (P("row", "col", None), P(), P(), P("row", "col", None))
    out_specs = (P("row", "col", None), P("row", "col", None), P())
    return jax.shard_map(body, mesh=mesh, in_specs=in_specs, out_specs=out_specs, check_vma=False)
```
